32 devices in a mesh: cell: 8 (over y, x, core), img: 4 (over z).
Axes of the slice: x: 2, y: 2, z: 4, core: 2. Of those that a mesh axis runs over, the one named last changes fastest.
Arguments:
- jac_cam: float32 [18, 262144], P(None, ('cell', 'img')), may hold values from -0.75 to 0.75
- jac_pt: float32 [6, 262144], P(None, ('cell', 'img')), may hold values from -6 to 6
- obs_residual: float32 [2, 262144], P(None, ('cell', 'img')), may hold values from -6 to 6
- obs_point: int32 [262144], P(('cell', 'img')), may hold values from 0 to 1023
- obs_slot: int32 [262144], P(('cell', 'img')), may hold values from 0 to 2047
- request: int32 [1024, 64], P(('cell', 'img')), may hold values from 0 to 767, as said below
- obs_count: int32 [32], P(('cell', 'img')), may hold values from 4096 to 8192, as said below
- cam_damp: float32 [9, 24576], P(None, ('cell', 'img')), may hold values from 0.16 to 2
- pt_damp: float32 [32768], P(('cell', 'img')), may hold values from 1 to 8
Outputs:
- camera_update: float32 [9, 24576], P(None, ('cell', 'img'))
- camera_residual: float32 [9, 24576], P(None, ('cell', 'img'))
The draws below stay inside these ranges and needn't reach their ends.
Inputs may be any that keep to these rules, and one draw needn't show every extreme that they name: obs_point indexes the observation's device's block of 1024 points. `obs_slot`: slot s of a device names column s % 64 of its request row s // 64. `request`: row w of a device's 32 rows lists 64 different cameras of owner device w, as indices within that owner's 768 cameras. `obs_count`: some device has all 8192 slots live.
All inputs are finite; a program needn't handle non-finite values.
Results may differ from the reference program's by a relative error of at most 0.00016.
Values sent between devices are 32-bit elements; how exact they have to be, the bound alone decides.
No kernel may reach another device: no remote copies, remote signals or barrier semaphores. Data moves between devices by JAX's collectives and lax.ppermute only.
A program may use at most 128 MiB of HBM per device.

```python
import math
import jax
import jax.numpy as jnp

CAM_DEV = 768
OBS_DEV = 8192
CAP = 64
ITERS = 2
PTS_DEV = 1024
SHARDS = 32
NCAM = 24576
NPTS = 32768
NOBS = 262144


def draw_request(key, part):
    row_keys = jax.random.split(key, SHARDS * SHARDS)
    return jax.vmap(lambda row_key: jax.random.permutation(row_key, CAM_DEV)[:CAP])(row_keys).astype(jnp.int32)


def draw_obs_count(key, part):
    count_key = jax.random.fold_in(key, 11)
    full_key = jax.random.fold_in(key, 12)
    counts = jax.random.randint(count_key, (SHARDS,), OBS_DEV // 2, OBS_DEV + 1).astype(jnp.int32)
    full_device = jax.random.randint(full_key, (), 0, SHARDS)
    return counts.at[full_device].set(OBS_DEV).astype(jnp.int32)


def draw_cam_damp(key, part):
    owner = (jnp.arange(NCAM) // CAM_DEV).astype(jnp.float32)
    factor = 1.0 / (1.0 + 2.0 * owner / max(SHARDS - 1, 1))
    base = jnp.exp(jax.random.uniform(key, (9, NCAM), jnp.float32, math.log(0.5), math.log(2.0)))
    return (base * factor[None]).astype(jnp.float32)


def set_ends(result, stream_key, least, top_value):
    place = [jax.random.randint(jax.random.fold_in(stream_key, axis), (), 0, length) for axis, length in enumerate(result.shape)]
    main_axis = result.shape.index(max(result.shape))
    beside = place[:main_axis] + [(place[main_axis] + 1) % result.shape[main_axis]] + place[main_axis + 1:]
    return result.at[tuple(place)].set(least).at[tuple(beside)].set(top_value)


def steps_of(own_key, dims, pieces, low, high):
    def one(dim, parts):
        steps = jax.random.uniform(jax.random.fold_in(jax.random.fold_in(own_key, 6), dim), (parts,), jnp.float32, low / len(pieces), high / len(pieces))
        return jnp.repeat(jnp.exp(steps), dims[dim] // parts).reshape((-1,) + (1,) * (len(dims) - dim - 1))

    level = one(*pieces[0])
    for cut in pieces[1:]:
        level = level * one(*cut)
    return level


def noise(stream_key, extent, scale, limit, shards=(), kind=jnp.bfloat16):
    values = jax.random.normal(stream_key, extent, jnp.float32) * scale
    if len(shards) > 0:
        values = steps_of(stream_key, extent, shards, -0.22, 0.18) * values
    return jnp.clip(values, min=-limit, max=limit).astype(kind)


def setup_inputs(seed: int = 0) -> dict:
    streams_of = jax.random.split(jax.random.key(seed), 10)
    return {
        "jac_cam": noise(streams_of[0], (18, NOBS), 0.125, 0.75, ((1, 32),), jnp.float32),
        "jac_pt": noise(streams_of[1], (6, NOBS), 1.0, 6.0, ((1, 32),), jnp.float32),
        "obs_residual": noise(streams_of[2], (2, NOBS), 1.0, 6.0, ((1, 32),), jnp.float32),
        "obs_point": set_ends(jax.random.randint(streams_of[3], (NOBS,), 0, PTS_DEV), jax.random.fold_in(streams_of[3], 1), 0, PTS_DEV - 1).astype(jnp.int32),
        "obs_slot": set_ends(jax.random.randint(streams_of[4], (NOBS,), 0, SHARDS * CAP), jax.random.fold_in(streams_of[4], 1), 0, (SHARDS * CAP) - 1).astype(jnp.int32),
        "request": draw_request(jax.random.fold_in(streams_of[9], 71), 0),
        "obs_count": draw_obs_count(jax.random.fold_in(streams_of[9], 71), 0),
        "cam_damp": draw_cam_damp(jax.random.fold_in(streams_of[9], 71), 0),
        "pt_damp": jnp.clip(jnp.exp(math.log(8.0) - 2.0794415 * jax.random.uniform(streams_of[8], (NPTS,), jnp.float32) ** steps_of(streams_of[8], (NPTS,), ((0, 32),), -0.2, 0.2)), 1.0, 8.0),
    }


def point_inverse(jac_pt, point_ids, pt_damp):
    npoints = pt_damp.shape[0]
    rows_a = jac_pt[0:3]
    rows_b = jac_pt[3:6]
    products = rows_a[:, None] * rows_a[None] + rows_b[:, None] * rows_b[None]
    matrix = jnp.zeros((3, 3, npoints), jnp.float32).at[:, :, point_ids].add(products)
    matrix = matrix + jnp.eye(3, dtype=jnp.float32)[:, :, None] * pt_damp[None, None]
    cofactor = [[matrix[(row_index + 1) % 3, (col_index + 1) % 3] * matrix[(row_index + 2) % 3, (col_index + 2) % 3]
                 - matrix[(row_index + 1) % 3, (col_index + 2) % 3] * matrix[(row_index + 2) % 3, (col_index + 1) % 3]
                 for col_index in range(3)] for row_index in range(3)]
    determinant = matrix[0, 0] * cofactor[0][0] + matrix[0, 1] * cofactor[0][1] + matrix[0, 2] * cofactor[0][2]
    adjugate = jnp.stack([jnp.stack([cofactor[col_index][row_index] for col_index in range(3)]) for row_index in range(3)])
    return adjugate / determinant[None, None]


def reduce_part(jac_pt, point_ids, inverse, along_first, along_second):
    rows_a = jac_pt[0:3]
    rows_b = jac_pt[3:6]
    projected = rows_a * along_first[None] + rows_b * along_second[None]
    npoints = inverse.shape[2]
    totals = jnp.zeros((3, npoints), jnp.float32).at[:, point_ids].add(projected)
    solved = jnp.sum(inverse * totals[None], axis=1)
    spread = solved[:, point_ids]
    return along_first - jnp.sum(rows_a * spread, axis=0), along_second - jnp.sum(rows_b * spread, axis=0)


def camera_terms(jac_cam, jac_pt, point_ids, inverse, values):
    along_first = jnp.sum(jac_cam[:9] * values, axis=0)
    along_second = jnp.sum(jac_cam[9:] * values, axis=0)
    kept_first, kept_second = reduce_part(jac_pt, point_ids, inverse, along_first, along_second)
    return jac_cam[:9] * kept_first[None] + jac_cam[9:] * kept_second[None]


def reference(jac_cam, jac_pt, obs_residual, obs_point, obs_slot, request, obs_count, cam_damp, pt_damp):
    obs_total = jac_cam.shape[1]
    position = jnp.arange(obs_total, dtype=jnp.int32)
    device = (position // OBS_DEV).astype(jnp.int32)
    live_mask = ((position % OBS_DEV) < obs_count[device]).astype(jnp.float32)
    jac_cam = jac_cam * live_mask[None]
    jac_pt = jac_pt * live_mask[None]
    obs_residual = obs_residual * live_mask[None]
    point_ids = (device * PTS_DEV + obs_point).astype(jnp.int32)
    owner = (obs_slot // CAP).astype(jnp.int32)
    camera_ids = (owner * CAM_DEV + request[device * SHARDS + owner, obs_slot % CAP]).astype(jnp.int32)
    inverse = point_inverse(jac_pt, point_ids, pt_damp)

    def to_cameras(per_obs):
        return jnp.zeros((per_obs.shape[0], NCAM), jnp.float32).at[:, camera_ids].add(per_obs)

    def apply_schur(direction):
        obs_terms = camera_terms(jac_cam, jac_pt, point_ids, inverse, direction[:, camera_ids])
        return to_cameras(obs_terms) + cam_damp * direction

    kept_first, kept_second = reduce_part(jac_pt, point_ids, inverse, obs_residual[0], obs_residual[1])
    rhs_terms = -(jac_cam[:9] * kept_first[None] + jac_cam[9:] * kept_second[None])
    diag_terms = jac_cam[:9] * jac_cam[:9] + jac_cam[9:] * jac_cam[9:]
    residual = to_cameras(rhs_terms)
    scaling = to_cameras(diag_terms) + cam_damp
    update = jnp.zeros_like(residual)
    precond = residual / scaling
    direction = precond
    inner_now = jnp.sum(residual * precond)
    for iteration in range(ITERS):
        schur_image = apply_schur(direction)
        step_size = inner_now / jnp.sum(direction * schur_image)
        update = update + step_size * direction
        residual = residual - step_size * schur_image
        if iteration + 1 < ITERS:
            precond = residual / scaling
            inner_next = jnp.sum(residual * precond)
            direction = precond + (inner_next / inner_now) * direction
            inner_now = inner_next
    return update, residual
```

```python
import functools

import jax
import jax.numpy as jnp
from jax import lax
from jax.experimental import pallas as pl
from jax.experimental.pallas import tpu as pltpu
from jax.sharding import PartitionSpec as P

AXES = ("cell", "img")
F32 = jnp.float32
BF16 = jnp.bfloat16
LANES = 128
CAP = 64
VMEM_BYTES = 48 * 1024 * 1024


def iota(shape, dim):
    return lax.broadcasted_iota(jnp.int32, shape, dim)


def take_lanes(table, lanes):
    return jnp.take_along_axis(table, lanes, axis=1, mode="promise_in_bounds")


def contract(left, right):
    return lax.dot_general(left, right, (((1,), (1,)), ((), ())), preferred_element_type=F32)


def one_hot_rows(index, rows):
    hit = iota((rows, index.shape[1]), 0) == index
    return jnp.where(hit, 1.0, 0.0).astype(BF16)


def rounded_parts(value, count):
    parts = []
    for _ in range(count):
        part = value.astype(BF16)
        parts.append(part)
        value = value - part.astype(F32)
    return parts


def spread_groups(tiles, group, groups):
    rows = []
    width = group.shape[1]
    for number in range(groups):
        hit = jnp.where(jnp.broadcast_to(group, (16, width)) == number, 1.0, 0.0).astype(BF16)
        rows += [tile * hit for tile in tiles]
    return jnp.concatenate(rows, axis=0)


def swap_halves(value):
    return pltpu.roll(value, CAP, 1)


def unpack_pair(even, odd):
    left = iota((8, LANES), 1) < CAP
    return jnp.where(left, even, swap_halves(odd)), jnp.where(left, swap_halves(even), odd)


def pack_pair(low, high):
    left = iota((8, LANES), 1) < CAP
    return jnp.where(left, low, swap_halves(high)), jnp.where(left, swap_halves(low), high)


def scalar_spot():
    return (iota((8, LANES), 0) == 1) & (iota((8, LANES), 1) >= CAP)


def sum_all(value):
    return jnp.sum(jnp.sum(value, axis=1, keepdims=True), axis=0, keepdims=True)


def carried_scalar(ref):
    total = ref[0]
    for sender in range(1, ref.shape[0]):
        total = total + ref[sender]
    return total[1:2, CAP:CAP + 1]


def store_pairs(out_ref, sums_ref, rows_each, offset, top, scalar):
    width = sums_ref.shape[1]
    for group in range(sums_ref.shape[0] // rows_each):
        start = group * rows_each + offset
        block = sums_ref[start:start + 16, :] + sums_ref[start + 16:start + 32, :]
        for part in range(width // LANES):
            pair = group * (width // LANES) + part
            lanes = slice(part * LANES, (part + 1) * LANES)
            even, odd = pack_pair(block[0:8, lanes], block[8:16, lanes])
            if scalar is not None:
                even = jnp.where(scalar_spot(), scalar, even)
                odd = jnp.where(scalar_spot(), scalar, odd)
            out_ref[2 * pair, top:top + 8] = even
            out_ref[2 * pair + 1, top:top + 8] = odd


def point_spread(solved_ref, point, jac_a, jac_b):
    low = jnp.broadcast_to(point & (LANES - 1), (8, LANES))
    hit = jnp.broadcast_to(point >> 7, (8, LANES)) == iota((8, LANES), 0)
    first = jnp.zeros((8, LANES), F32)
    second = jnp.zeros((8, LANES), F32)
    for axis in range(3):
        taken = jnp.where(hit, take_lanes(solved_ref[axis], low), 0.0)
        first = first + jac_a[axis:axis + 1] * taken
        second = second + jac_b[axis:axis + 1] * taken
    return jnp.sum(first, axis=0, keepdims=True), jnp.sum(second, axis=0, keepdims=True)


def live_group(index, shift, start, count):
    spot = iota(index.shape, 1) + start
    return jnp.where(spot < count, index >> shift, -1)


def solve_points(inverse_ref, totals, solved_ref):
    rows = ((0, 3, 5), (3, 1, 4), (5, 4, 2))
    for axis in range(3):
        solved_ref[axis] = (
            inverse_ref[rows[axis][0]] * totals[0]
            + inverse_ref[rows[axis][1]] * totals[1]
            + inverse_ref[rows[axis][2]] * totals[2]
        )


def start_kernel(chunk, count_ref, cam_ref, pt_ref, err_ref, point_ref, slot_ref, req_ref, damp_ref,
                 out_ref, camp_ref, pta_ref, ptb_ref, inverse_ref, psum_ref, ssum_ref, solved_ref):
    nobs = cam_ref.shape[1]
    count = count_ref[0]
    psum_ref[...] = jnp.zeros_like(psum_ref)
    ssum_ref[...] = jnp.zeros_like(ssum_ref)
    groups = ssum_ref.shape[0] // 64

    def gather_points(step, carry):
        start = pl.multiple_of(step * chunk, chunk)
        lanes = pl.ds(start, chunk)
        point = point_ref[:, lanes]
        jac = pt_ref[:, lanes]
        zero = jnp.zeros((1, chunk), F32)
        jac_a = jnp.concatenate([jac[0:3], zero, jac[0:3], zero], axis=0)
        jac_b = jnp.concatenate([jac[3:6], zero, jac[3:6], zero], axis=0)
        pta_ref[:, lanes] = jac_a
        ptb_ref[:, lanes] = jac_b
        turn_a = jnp.concatenate([jac[0:3], zero, jac[1:3], jac[0:1], zero], axis=0)
        turn_b = jnp.concatenate([jac[3:6], zero, jac[4:6], jac[3:4], zero], axis=0)
        err = err_ref[:, lanes]
        blocks = jac_a * turn_a + jac_b * turn_b
        sides = jac_a * err[0:1] + jac_b * err[1:2]
        tiles = rounded_parts(jnp.concatenate([blocks, sides], axis=0), 3)
        spread = spread_groups(tiles, live_group(point, 7, start, count), 8)
        psum_ref[...] += contract(spread, one_hot_rows(point & (LANES - 1), LANES))
        return carry

    lax.fori_loop(0, nobs // chunk, gather_points, 0)

    def row(number):
        total = psum_ref[pl.ds(number, 8, stride=48), :]
        total = total + psum_ref[pl.ds(number + 16, 8, stride=48), :]
        return total + psum_ref[pl.ds(number + 32, 8, stride=48), :]

    damp = damp_ref[...]
    m00, m11, m22 = row(0) + damp, row(1) + damp, row(2) + damp
    m01, m12, m20 = row(4), row(5), row(6)
    c00 = m11 * m22 - m12 * m12
    c01 = m12 * m20 - m01 * m22
    c02 = m01 * m12 - m11 * m20
    c11 = m22 * m00 - m20 * m20
    c12 = m20 * m01 - m12 * m00
    c22 = m00 * m11 - m01 * m01
    det = m00 * c00 + m01 * c01 + m20 * c02
    for place, cofactor in enumerate((c00, c11, c22, c01, c12, c02)):
        inverse_ref[place] = cofactor / det
    solve_points(inverse_ref, [row(8), row(9), row(10)], solved_ref)

    def scatter_terms(step, carry):
        start = pl.multiple_of(step * chunk, chunk)
        lanes = pl.ds(start, chunk)
        slot = slot_ref[:, lanes]
        camp_ref[0:9, lanes] = cam_ref[0:9, lanes]
        camp_ref[9:16, lanes] = jnp.zeros((7, chunk), F32)
        camp_ref[16:25, lanes] = cam_ref[9:18, lanes]
        camp_ref[25:32, lanes] = jnp.zeros((7, chunk), F32)
        kept_a, kept_b = [], []
        for tile in range(chunk // LANES):
            spot = pl.ds(start + tile * LANES, LANES)
            first, second = point_spread(solved_ref, point_ref[:, spot], pta_ref[:, spot], ptb_ref[:, spot])
            err = err_ref[:, spot]
            kept_a.append(err[0:1] - first)
            kept_b.append(err[1:2] - second)
        kept_a = jnp.concatenate(kept_a, axis=1)
        kept_b = jnp.concatenate(kept_b, axis=1)
        cam_a = camp_ref[0:16, lanes]
        cam_b = camp_ref[16:32, lanes]
        rhs = -(cam_a * kept_a + cam_b * kept_b)
        diag = cam_a * cam_a + cam_b * cam_b
        tiles = rounded_parts(rhs, 2) + rounded_parts(diag, 2)
        spread = spread_groups(tiles, live_group(slot, 8, start, count), groups)
        ssum_ref[...] += contract(spread, one_hot_rows(slot & 255, 256))
        return carry

    lax.fori_loop(0, nobs // chunk, scatter_terms, 0)
    store_pairs(out_ref, ssum_ref, 64, 0, 0, None)
    store_pairs(out_ref, ssum_ref, 64, 32, 8, None)
    wanted = req_ref[...].astype(F32)
    wanted = jnp.concatenate([jnp.zeros_like(wanted), wanted], axis=1)
    for owner in range(req_ref.shape[0]):
        out_ref[owner, 8:16] = jnp.where(scalar_spot(), wanted[owner:owner + 1], out_ref[owner, 8:16])


def apply_kernel(chunk, first, *refs):
    if first:
        (count_ref, in_ref, camp_ref, pta_ref, ptb_ref, point_ref, slot_ref, inverse_ref, damp_ref, precond_ref,
         out_ref, table_ref, rz_ref, psum_ref, ssum_ref, solved_ref, along_ref, last_ref) = refs
    else:
        (count_ref, in_ref, camp_ref, pta_ref, ptb_ref, point_ref, slot_ref, inverse_ref, damp_ref, precond_ref,
         oldtable_ref, oldrz_ref, oldown_ref,
         out_ref, own_ref, rz_ref, psum_ref, ssum_ref, solved_ref, along_ref, last_ref, table_ref) = refs
    nobs = camp_ref.shape[1]
    count = count_ref[0]
    psum_ref[...] = jnp.zeros_like(psum_ref)
    ssum_ref[...] = jnp.zeros_like(ssum_ref)
    groups = ssum_ref.shape[0] // 32
    pairs = in_ref.shape[0] // 2
    rz = carried_scalar(in_ref)
    rz_ref[...] = jnp.broadcast_to(rz, rz_ref.shape)
    own = precond_ref[...]
    if not first:
        beta = rz / oldrz_ref[0:1, 0:1]
        own = own + beta * oldown_ref[...]
        own_ref[...] = own
    for pair in range(pairs):
        low, high = unpack_pair(in_ref[2 * pair], in_ref[2 * pair + 1])
        if not first:
            low = low + beta * oldtable_ref[pair, 0:8]
            high = high + beta * oldtable_ref[pair, 8:16]
        table_ref[pair, 0:8] = low
        table_ref[pair, 8:16] = high
        last_ref[pair:pair + 1, :] = high[0:1]

    def gather_points(step, carry):
        start = pl.multiple_of(step * chunk, chunk)
        lanes = pl.ds(start, chunk)
        for tile in range(chunk // LANES):
            spot = pl.ds(start + tile * LANES, LANES)
            slot = slot_ref[:, spot]
            low = jnp.broadcast_to(slot & (LANES - 1), (8, LANES))
            high = jnp.broadcast_to(slot >> 7, (8, LANES))
            taken = jnp.zeros((8, LANES), F32)
            for pair in range(pairs):
                taken = jnp.where(high == pair, take_lanes(table_ref[pair, 0:8], low), taken)
            tail = jnp.zeros((8, LANES), F32)
            for base in range(0, pairs, 8):
                hit = high == iota((8, LANES), 0) + base
                tail = jnp.where(hit, take_lanes(last_ref[base:base + 8], low), tail)
            tail = jnp.sum(tail, axis=0, keepdims=True)
            along_ref[0:1, spot] = jnp.sum(camp_ref[0:8, spot] * taken, axis=0, keepdims=True) + camp_ref[8:9, spot] * tail
            along_ref[1:2, spot] = jnp.sum(camp_ref[16:24, spot] * taken, axis=0, keepdims=True) + camp_ref[24:25, spot] * tail
        point = point_ref[:, lanes]
        sides = pta_ref[:, lanes] * along_ref[0:1, lanes] + ptb_ref[:, lanes] * along_ref[1:2, lanes]
        parts = rounded_parts(sides, 3)
        later = jnp.where(iota((8, chunk), 0) < 4, parts[1].astype(F32), parts[2].astype(F32))
        tile = jnp.concatenate([parts[0].astype(F32), later], axis=0).astype(BF16)
        spread = spread_groups([tile], live_group(point, 7, start, count), 8)
        psum_ref[...] += contract(spread, one_hot_rows(point & (LANES - 1), LANES))
        return carry

    lax.fori_loop(0, nobs // chunk, gather_points, 0)

    def row(number):
        total = psum_ref[pl.ds(number, 8, stride=16), :]
        total = total + psum_ref[pl.ds(number + 8, 8, stride=16), :]
        return total + psum_ref[pl.ds(number + 12, 8, stride=16), :]

    solve_points(inverse_ref, [row(0), row(1), row(2)], solved_ref)

    def scatter_terms(step, carry):
        start = pl.multiple_of(step * chunk, chunk)
        lanes = pl.ds(start, chunk)
        slot = slot_ref[:, lanes]
        kept_a, kept_b = [], []
        for tile in range(chunk // LANES):
            spot = pl.ds(start + tile * LANES, LANES)
            first_sum, second_sum = point_spread(solved_ref, point_ref[:, spot], pta_ref[:, spot], ptb_ref[:, spot])
            kept_a.append(along_ref[0:1, spot] - first_sum)
            kept_b.append(along_ref[1:2, spot] - second_sum)
        kept_a = jnp.concatenate(kept_a, axis=1)
        kept_b = jnp.concatenate(kept_b, axis=1)
        terms = camp_ref[0:16, lanes] * kept_a + camp_ref[16:32, lanes] * kept_b
        spread = spread_groups(rounded_parts(terms, 2), live_group(slot, 8, start, count), groups)
        ssum_ref[...] += contract(spread, one_hot_rows(slot & 255, 256))
        energy = along_ref[0:1, lanes] * kept_a + along_ref[1:2, lanes] * kept_b
        energy = jnp.where(iota((1, chunk), 1) + start < count, energy, 0.0)
        return carry + energy

    energy = lax.fori_loop(0, nobs // chunk, scatter_terms, jnp.zeros((1, chunk), F32))
    partial = sum_all(energy) + sum_all(damp_ref[...] * own * own)
    store_pairs(out_ref, ssum_ref, 32, 0, 0, partial)


def owner_sums(values, ids, cameras):
    groups = cameras // 256
    tiles = []
    for value in values:
        tiles += rounded_parts(value, 2)
    spread = spread_groups(tiles, ids >> 8, groups)
    sums = contract(spread, one_hot_rows(ids & 255, 256))
    results = []
    each = 16 * len(tiles)
    for place in range(len(values)):
        blocks = []
        for group in range(groups):
            start = group * each + place * 32
            blocks.append(sums[start:start + 16] + sums[start + 16:start + 32])
        results.append(jnp.concatenate(blocks, axis=1)[0:9])
    return results


def send_wanted(out_ref, precond, ids, scalar):
    cameras = precond.shape[1]
    pairs = out_ref.shape[0] // 2
    for pair in range(pairs):
        own = ids[:, pair * LANES:(pair + 1) * LANES]
        low = jnp.broadcast_to(own & (LANES - 1), (8, LANES))
        high = jnp.broadcast_to(own >> 7, (8, LANES))
        head = jnp.zeros((8, LANES), F32)
        tail = jnp.zeros((8, LANES), F32)
        for block in range(cameras // LANES):
            lanes = slice(block * LANES, (block + 1) * LANES)
            hit = high == block
            head = jnp.where(hit, take_lanes(precond[0:8, lanes], low), head)
            last = jnp.broadcast_to(precond[8:9, lanes], (8, LANES))
            tail = jnp.where(hit, take_lanes(last, low), tail)
        even, odd = pack_pair(head, tail)
        out_ref[2 * pair] = jnp.where(scalar_spot(), scalar, even)
        out_ref[2 * pair + 1] = jnp.where(scalar_spot(), scalar, odd)


def owner_start_kernel(in_ref, damp_ref, out_ref, residual_ref, scaling_ref, precond_ref, ids_ref):
    pairs = in_ref.shape[0] // 2
    rhs, diag, ids = [], [], []
    for pair in range(pairs):
        rhs.append(jnp.concatenate(unpack_pair(in_ref[2 * pair, 0:8], in_ref[2 * pair + 1, 0:8]), axis=0))
        low, high = unpack_pair(in_ref[2 * pair, 8:16], in_ref[2 * pair + 1, 8:16])
        diag.append(jnp.concatenate([low, high], axis=0))
        ids.append(high[1:2].astype(jnp.int32))
    ids = jnp.concatenate(ids, axis=1)
    ids_ref[...] = ids
    rhs = jnp.concatenate(rhs, axis=1)
    diag = jnp.concatenate(diag, axis=1)
    residual, diag = owner_sums([rhs, diag], ids, damp_ref.shape[1])
    scaling = diag + damp_ref[...]
    precond = residual / scaling
    residual_ref[...] = residual
    scaling_ref[...] = scaling
    precond_ref[...] = precond
    send_wanted(out_ref, precond, ids, sum_all(residual * precond))


def owner_image(in_ref, ids, cameras):
    image = []
    for pair in range(in_ref.shape[0] // 2):
        image.append(jnp.concatenate(unpack_pair(in_ref[2 * pair], in_ref[2 * pair + 1]), axis=0))
    return owner_sums([jnp.concatenate(image, axis=1)], ids, cameras)[0]


def owner_middle_kernel(in_ref, ids_ref, rz_ref, damp_ref, direction_ref, residual_ref, scaling_ref,
                        out_ref, update_ref, newres_ref, precond_ref):
    ids = ids_ref[...]
    direction = direction_ref[...]
    image = owner_image(in_ref, ids, damp_ref.shape[1]) + damp_ref[...] * direction
    step = rz_ref[0:1, 0:1] / carried_scalar(in_ref)
    update_ref[...] = step * direction
    residual = residual_ref[...] - step * image
    precond = residual / scaling_ref[...]
    newres_ref[...] = residual
    precond_ref[...] = precond
    send_wanted(out_ref, precond, ids, sum_all(residual * precond))


def owner_end_kernel(in_ref, ids_ref, rz_ref, damp_ref, direction_ref, residual_ref, update_ref,
                     newupdate_ref, newres_ref):
    direction = direction_ref[...]
    image = owner_image(in_ref, ids_ref[...], damp_ref.shape[1]) + damp_ref[...] * direction
    step = rz_ref[0:1, 0:1] / carried_scalar(in_ref)
    newupdate_ref[...] = update_ref[...] + step * direction
    newres_ref[...] = residual_ref[...] - step * image


def call(kernel, outs, scratch, smem, *args):
    whole = pl.BlockSpec(memory_space=pltpu.VMEM)
    specs = [pl.BlockSpec(memory_space=pltpu.SMEM) if place < smem else whole for place in range(len(args))]
    return pl.pallas_call(
        kernel,
        out_shape=[jax.ShapeDtypeStruct(shape, dtype) for shape, dtype in outs],
        in_specs=specs,
        out_specs=[whole] * len(outs),
        scratch_shapes=[pltpu.VMEM(shape, F32) for shape in scratch],
        compiler_params=pltpu.CompilerParams(vmem_limit_bytes=VMEM_BYTES),
    )(*args)


def exchange(blocks):
    return lax.all_to_all(blocks, AXES, split_axis=0, concat_axis=0, tiled=True)


def body(jac_cam, jac_pt, obs_residual, obs_point, obs_slot, request, obs_count, cam_damp, pt_damp):
    nobs = jac_cam.shape[1]
    shards = request.shape[0]
    cameras = cam_damp.shape[1]
    slots = shards * CAP
    chunk = 512
    point = obs_point.reshape(1, nobs)
    slot = obs_slot.reshape(1, nobs)
    damp_rows = pt_damp.reshape(8, LANES)
    own = ((9, cameras), F32)
    blocks = ((shards, 8, LANES), F32)
    groups = slots // 256
    sums, camp, pta, ptb, inverse = call(
        functools.partial(start_kernel, chunk),
        [((shards, 16, LANES), F32), ((32, nobs), F32), ((8, nobs), F32), ((8, nobs), F32), ((6, 8, LANES), F32)],
        [(8 * 48, LANES), (groups * 64, 256), (3, 8, LANES)],
        1, obs_count, jac_cam, jac_pt, obs_residual, point, slot, request, damp_rows)
    arrived = exchange(sums)
    send, residual, scaling, precond, ids = call(
        owner_start_kernel, [blocks, own, own, own, ((1, slots), jnp.int32)], [], 0, arrived, cam_damp)
    arrived = exchange(send)
    scratch = [(8 * 16, LANES), (groups * 32, 256), (3, 8, LANES), (8, nobs), (shards // 2, LANES)]
    scalar = ((8, LANES), F32)
    table = ((shards // 2, 16, LANES), F32)
    send, table_now, rz = call(
        functools.partial(apply_kernel, chunk, True), [blocks, table, scalar], scratch,
        1, obs_count, arrived, camp, pta, ptb, point, slot, inverse, cam_damp, precond)
    arrived = exchange(send)
    direction = precond
    send, update, residual, precond = call(
        owner_middle_kernel, [blocks, own, own, own], [], 0,
        arrived, ids, rz, cam_damp, direction, residual, scaling)
    arrived = exchange(send)
    send, direction, rz = call(
        functools.partial(apply_kernel, chunk, False), [blocks, own, scalar], scratch + [table[0]],
        1, obs_count, arrived, camp, pta, ptb, point, slot, inverse, cam_damp, precond, table_now, rz, direction)
    arrived = exchange(send)
    update, residual = call(
        owner_end_kernel, [own, own], [], 0, arrived, ids, rz, cam_damp, direction, residual, update)
    return update, residual


def solution(mesh):
    wide = P(None, AXES)
    flat = P(AXES)
    return jax.shard_map(
        body,
        mesh=mesh,
        in_specs=(wide, wide, wide, flat, flat, P(AXES, None), flat, wide, flat),
        out_specs=(wide, wide),
        check_vma=False,
    )
```

```python
import functools

import jax
import jax.numpy as jnp
from jax import lax
from jax.experimental import pallas as pl
from jax.experimental.pallas import tpu as pltpu
from jax.sharding import PartitionSpec as P

AXES = ("cell", "img")
F32 = jnp.float32
BF16 = jnp.bfloat16
LANES = 128
CAP = 64
VMEM_BYTES = 48 * 1024 * 1024


def iota(shape, dim):
    return lax.broadcasted_iota(jnp.int32, shape, dim)


def take_lanes(table, lanes):
    return jnp.take_along_axis(table, lanes, axis=1, mode="promise_in_bounds")


def contract(left, right):
    return lax.dot_general(left, right, (((1,), (1,)), ((), ())), preferred_element_type=F32)


def one_hot_rows(index, rows):
    hit = iota((rows, index.shape[1]), 0) == index
    return jnp.where(hit, 1.0, 0.0).astype(BF16)


def rounded_parts(value, count):
    parts = []
    for _ in range(count):
        part = value.astype(BF16)
        parts.append(part)
        value = value - part.astype(F32)
    return parts


def masked_rows(rows, hit):
    return [jnp.where(hit, jnp.broadcast_to(row, hit.shape), 0.0) for row in rows]


def stack_tiles(blocks):
    if len(blocks) % 2:
        blocks = blocks + [jnp.zeros_like(blocks[0])]
    return jnp.concatenate(blocks, axis=0).astype(BF16)


def group_hits(group):
    return jnp.broadcast_to(group, (8, group.shape[1])) == iota((8, group.shape[1]), 0)


def spread_slots(heads, tails, group, groups):
    width = group.shape[1]
    tiles = [jnp.concatenate(parts, axis=0).astype(BF16) for parts in heads]
    rows = []
    wide = jnp.broadcast_to(group, (8, width))
    for number in range(groups):
        hit = jnp.where(wide == number, 1.0, 0.0)
        hit = jnp.concatenate([hit, hit], axis=0).astype(BF16)
        rows += [tile * hit for tile in tiles]
    last = []
    for base in range(0, groups, 8):
        hit = wide == iota((8, width), 0) + base
        last += masked_rows(tails, hit)
    return jnp.concatenate(rows + [stack_tiles(last)], axis=0)


def wide_parts(value, count):
    return [part.astype(F32) for part in rounded_parts(value, count)]


def swap_halves(value):
    return pltpu.roll(value, CAP, 1)


def left_half(rows=8):
    return iota((rows, LANES), 1) < CAP


def sum_all(value):
    return jnp.sum(jnp.sum(value, axis=1, keepdims=True), axis=0, keepdims=True)


def carried_scalar(ref):
    total = ref[4:5, :]
    for sender in range(1, ref.shape[0] // 5):
        total = total + ref[5 * sender + 4:5 * sender + 5, :]
    return total[:, CAP:CAP + 1]


def store_five(out_ref, pair, head, tail, scalar):
    left = left_half()
    turned = swap_halves(head)
    even = jnp.where(left, head, pltpu.roll(turned, 4, 0))
    odd = jnp.where(left, turned, pltpu.roll(head, 4, 0))
    last = jnp.broadcast_to(tail, (8, LANES))
    last_even = jnp.where(left, last, scalar)
    last_odd = jnp.where(left, swap_halves(last), scalar)
    out_ref[10 * pair:10 * pair + 4] = even[0:4]
    out_ref[10 * pair + 4:10 * pair + 5] = last_even[0:1]
    out_ref[10 * pair + 5:10 * pair + 9] = odd[0:4]
    out_ref[10 * pair + 9:10 * pair + 10] = last_odd[0:1]


def load_five(in_ref, pair):
    left = left_half(4)
    even = in_ref[10 * pair:10 * pair + 4]
    odd = in_ref[10 * pair + 5:10 * pair + 9]
    low = jnp.where(left, even, swap_halves(odd))
    high = jnp.where(left, swap_halves(even), odd)
    last_even = in_ref[10 * pair + 4:10 * pair + 5]
    last_odd = in_ref[10 * pair + 9:10 * pair + 10]
    tail = jnp.where(left_half(1), last_even, swap_halves(last_odd))
    return jnp.concatenate([low, high], axis=0), tail


def point_spread(solved_ref, low, group, jac_a, jac_b):
    low = jnp.broadcast_to(low, (8, LANES))
    hit = group_hits(group)
    first = jnp.zeros((8, LANES), F32)
    second = jnp.zeros((8, LANES), F32)
    for axis in range(3):
        taken = jnp.where(hit, take_lanes(solved_ref[axis], low), 0.0)
        first = first + jac_a[axis:axis + 1] * taken
        second = second + jac_b[axis:axis + 1] * taken
    return jnp.sum(first, axis=0, keepdims=True), jnp.sum(second, axis=0, keepdims=True)


def solve_points(inverse_ref, totals, solved_ref):
    rows = ((0, 3, 5), (3, 1, 4), (5, 4, 2))
    for axis in range(3):
        solved_ref[axis] = (
            inverse_ref[rows[axis][0]] * totals[0]
            + inverse_ref[rows[axis][1]] * totals[1]
            + inverse_ref[rows[axis][2]] * totals[2]
        )


def summed_parts(sums_ref, start, rows, count, step):
    total = sums_ref[start:start + rows, :]
    for part in range(1, count):
        begin = start + part * step
        total = total + sums_ref[begin:begin + rows, :]
    return total


def start_kernel(chunk, count_ref, cam_hbm, pt_hbm, err_hbm, point_hbm, slot_hbm, req_hbm, damp_hbm,
                 out_ref, camp_ref, pta_ref, ptb_ref, index_ref, inverse_ref,
                 psum_ref, ssum_ref, solved_ref, cam_ref, pt_ref, err_ref, point_ref, slot_ref, req_ref, damp_ref,
                 cam_sem, pt_sem, err_sem, point_sem, slot_sem, req_sem, damp_sem):
    nobs = cam_ref.shape[1]
    copies = [
        pltpu.make_async_copy(pt_hbm, pt_ref, pt_sem),
        pltpu.make_async_copy(err_hbm, err_ref, err_sem),
        pltpu.make_async_copy(point_hbm, point_ref, point_sem),
        pltpu.make_async_copy(slot_hbm, slot_ref, slot_sem),
        pltpu.make_async_copy(damp_hbm, damp_ref, damp_sem),
        pltpu.make_async_copy(cam_hbm, cam_ref, cam_sem),
        pltpu.make_async_copy(req_hbm, req_ref, req_sem),
    ]
    for copy in copies:
        copy.start()
    count = count_ref[0]
    psum_ref[...] = jnp.zeros_like(psum_ref)
    ssum_ref[...] = jnp.zeros_like(ssum_ref)
    groups = req_ref.shape[0] * CAP // 256
    for copy in copies[:5]:
        copy.wait()

    def gather_points(step, carry):
        start = pl.multiple_of(step * chunk, chunk)
        lanes = pl.ds(start, chunk)
        live = iota((1, chunk), 1) + start < count
        point = point_ref[:, lanes]
        low = point & (LANES - 1)
        group = jnp.where(live, point >> 7, -1)
        slot = slot_ref[:, lanes]
        index_ref[0:1, lanes] = low
        index_ref[1:2, lanes] = group
        index_ref[2:3, lanes] = slot
        index_ref[3:4, lanes] = jnp.where(live, slot >> 8, -1)
        jac = pt_ref[:, lanes]
        zero = jnp.zeros((1, chunk), F32)
        jac_a = jnp.concatenate([jac[0:3], zero, jac[0:3], zero], axis=0)
        jac_b = jnp.concatenate([jac[3:6], zero, jac[3:6], zero], axis=0)
        pta_ref[:, lanes] = jac_a
        ptb_ref[:, lanes] = jac_b
        turn_a = jnp.concatenate([jac[0:3], zero, jac[1:3], jac[0:1], zero], axis=0)
        turn_b = jnp.concatenate([jac[3:6], zero, jac[4:6], jac[3:4], zero], axis=0)
        err = err_ref[:, lanes]
        blocks = wide_parts(jac_a * turn_a + jac_b * turn_b, 3)
        sides = wide_parts(jac_a * err[0:1] + jac_b * err[1:2], 3)
        rows = [block[place:place + 1] for block in blocks for place in (0, 1, 2, 4, 5, 6)]
        rows += [side[place:place + 1] for side in sides for place in (0, 1, 2)]
        spread = stack_tiles(masked_rows(rows, group_hits(group)))
        psum_ref[...] += contract(spread, one_hot_rows(low, LANES))
        return carry

    lax.fori_loop(0, nobs // chunk, gather_points, 0)

    damp = damp_ref[...]
    m00, m11, m22, m01, m12, m20 = [summed_parts(psum_ref, 8 * place, 8, 3, 48) for place in range(6)]
    m00, m11, m22 = m00 + damp, m11 + damp, m22 + damp
    c00 = m11 * m22 - m12 * m12
    c01 = m12 * m20 - m01 * m22
    c02 = m01 * m12 - m11 * m20
    c11 = m22 * m00 - m20 * m20
    c12 = m20 * m01 - m12 * m00
    c22 = m00 * m11 - m01 * m01
    det = m00 * c00 + m01 * c01 + m20 * c02
    for place, cofactor in enumerate((c00, c11, c22, c01, c12, c02)):
        inverse_ref[place] = cofactor / det
    solve_points(inverse_ref, [summed_parts(psum_ref, 144 + 8 * place, 8, 3, 24) for place in range(3)], solved_ref)
    for copy in copies[5:]:
        copy.wait()

    def scatter_terms(step, carry):
        start = pl.multiple_of(step * chunk, chunk)
        lanes = pl.ds(start, chunk)
        camp_ref[0:9, lanes] = cam_ref[0:9, lanes]
        camp_ref[9:16, lanes] = jnp.zeros((7, chunk), F32)
        camp_ref[16:25, lanes] = cam_ref[9:18, lanes]
        camp_ref[25:32, lanes] = jnp.zeros((7, chunk), F32)
        kept_a, kept_b = [], []
        for tile in range(chunk // LANES):
            spot = pl.ds(start + tile * LANES, LANES)
            first, second = point_spread(
                solved_ref, index_ref[0:1, spot], index_ref[1:2, spot], pta_ref[:, spot], ptb_ref[:, spot])
            err = err_ref[:, spot]
            kept_a.append(err[0:1] - first)
            kept_b.append(err[1:2] - second)
        kept_a = jnp.concatenate(kept_a, axis=1)
        kept_b = jnp.concatenate(kept_b, axis=1)
        cam_a = camp_ref[0:16, lanes]
        cam_b = camp_ref[16:32, lanes]
        rhs = wide_parts(-(cam_a * kept_a + cam_b * kept_b), 2)
        diag = wide_parts(cam_a * cam_a + cam_b * cam_b, 2)
        heads = [[part[0:8] for part in rhs], [part[0:8] for part in diag]]
        tails = [part[8:9] for part in rhs + diag]
        slot = index_ref[2:3, lanes]
        spread = spread_slots(heads, tails, index_ref[3:4, lanes], groups)
        ssum_ref[...] += contract(spread, one_hot_rows(slot & 255, 256))
        return carry

    lax.fori_loop(0, nobs // chunk, scatter_terms, 0)
    wanted = req_ref[...].astype(F32)
    wanted = jnp.concatenate([wanted, jnp.zeros_like(wanted)], axis=1)
    left = left_half()
    for group in range(groups):
        rhs = summed_parts(ssum_ref, 32 * group, 8, 2, 8)
        diag = summed_parts(ssum_ref, 32 * group + 16, 8, 2, 8)
        last = 32 * groups + 32 * (group // 8) + group % 8
        rhs_last = summed_parts(ssum_ref, last, 1, 2, 8)
        diag_last = summed_parts(ssum_ref, last + 16, 1, 2, 8)
        for half in range(2):
            lanes = slice(half * LANES, (half + 1) * LANES)
            row = 20 * (2 * group + half)
            out_ref[row:row + 8] = jnp.where(left, rhs[:, lanes], swap_halves(diag[:, lanes]))
            out_ref[row + 10:row + 18] = jnp.where(left, swap_halves(rhs[:, lanes]), diag[:, lanes])
            left_one = left_half(1)
            out_ref[row + 8:row + 9] = jnp.where(left_one, rhs_last[:, lanes], swap_halves(diag_last[:, lanes]))
            out_ref[row + 18:row + 19] = jnp.where(left_one, swap_halves(rhs_last[:, lanes]), diag_last[:, lanes])
            owner = 4 * group + 2 * half
            out_ref[row + 9:row + 10] = wanted[owner:owner + 1]
            out_ref[row + 19:row + 20] = wanted[owner + 1:owner + 2]


def apply_kernel(chunk, first, *refs):
    if first:
        (in_ref, camp_ref, pta_ref, ptb_ref, index_ref, inverse_ref, damp_ref, precond_ref,
         out_ref, table_ref, last_ref, rz_ref, psum_ref, ssum_ref, solved_ref, along_ref) = refs
    else:
        (in_ref, camp_ref, pta_ref, ptb_ref, index_ref, inverse_ref, damp_ref, precond_ref,
         oldtable_ref, oldlast_ref, oldrz_ref, oldown_ref,
         out_ref, own_ref, rz_ref, psum_ref, ssum_ref, solved_ref, along_ref, table_ref, last_ref) = refs
    nobs = camp_ref.shape[1]
    psum_ref[...] = jnp.zeros_like(psum_ref)
    ssum_ref[...] = jnp.zeros_like(ssum_ref)
    pairs = table_ref.shape[0]
    groups = pairs // 2
    rz = carried_scalar(in_ref)
    rz_ref[...] = jnp.broadcast_to(rz, rz_ref.shape)
    own = precond_ref[...]
    if not first:
        beta = rz / oldrz_ref[0:1, 0:1]
        own = own + beta * oldown_ref[...]
        own_ref[...] = own
    for pair in range(pairs):
        head, tail = load_five(in_ref, pair)
        if not first:
            head = head + beta * oldtable_ref[pair]
            tail = tail + beta * oldlast_ref[pair:pair + 1]
        table_ref[pair] = head
        last_ref[pair:pair + 1] = tail

    def gather_points(step, carry):
        start = pl.multiple_of(step * chunk, chunk)
        lanes = pl.ds(start, chunk)
        for tile in range(chunk // LANES):
            spot = pl.ds(start + tile * LANES, LANES)
            slot = index_ref[2:3, spot]
            low = jnp.broadcast_to(slot & (LANES - 1), (8, LANES))
            high = jnp.broadcast_to(slot >> 7, (8, LANES))
            taken = jnp.zeros((8, LANES), F32)
            for pair in range(pairs):
                taken = jnp.where(high == pair, take_lanes(table_ref[pair], low), taken)
            tail = jnp.zeros((8, LANES), F32)
            for base in range(0, pairs, 8):
                hit = high == iota((8, LANES), 0) + base
                tail = jnp.where(hit, take_lanes(last_ref[base:base + 8], low), tail)
            tail = jnp.sum(tail, axis=0, keepdims=True)
            along_ref[0:1, spot] = jnp.sum(camp_ref[0:8, spot] * taken, axis=0, keepdims=True) + camp_ref[8:9, spot] * tail
            along_ref[1:2, spot] = jnp.sum(camp_ref[16:24, spot] * taken, axis=0, keepdims=True) + camp_ref[24:25, spot] * tail
        sides = wide_parts(pta_ref[:, lanes] * along_ref[0:1, lanes] + ptb_ref[:, lanes] * along_ref[1:2, lanes], 3)
        rows = [side[place:place + 1] for side in sides for place in (0, 1, 2)]
        spread = stack_tiles(masked_rows(rows, group_hits(index_ref[1:2, lanes])))
        psum_ref[...] += contract(spread, one_hot_rows(index_ref[0:1, lanes], LANES))
        return carry

    lax.fori_loop(0, nobs // chunk, gather_points, 0)
    solve_points(inverse_ref, [summed_parts(psum_ref, 8 * place, 8, 3, 24) for place in range(3)], solved_ref)

    def scatter_terms(step, carry):
        start = pl.multiple_of(step * chunk, chunk)
        lanes = pl.ds(start, chunk)
        kept_a, kept_b = [], []
        for tile in range(chunk // LANES):
            spot = pl.ds(start + tile * LANES, LANES)
            first_sum, second_sum = point_spread(
                solved_ref, index_ref[0:1, spot], index_ref[1:2, spot], pta_ref[:, spot], ptb_ref[:, spot])
            kept_a.append(along_ref[0:1, spot] - first_sum)
            kept_b.append(along_ref[1:2, spot] - second_sum)
        kept_a = jnp.concatenate(kept_a, axis=1)
        kept_b = jnp.concatenate(kept_b, axis=1)
        terms = wide_parts(camp_ref[0:16, lanes] * kept_a + camp_ref[16:32, lanes] * kept_b, 2)
        group = index_ref[3:4, lanes]
        spread = spread_slots([[part[0:8] for part in terms]], [part[8:9] for part in terms], group, groups)
        ssum_ref[...] += contract(spread, one_hot_rows(index_ref[2:3, lanes] & 255, 256))
        energy = along_ref[0:1, lanes] * kept_a + along_ref[1:2, lanes] * kept_b
        return carry + jnp.where(group >= 0, energy, 0.0)

    energy = lax.fori_loop(0, nobs // chunk, scatter_terms, jnp.zeros((1, chunk), F32))
    partial = sum_all(energy) + sum_all(damp_ref[...] * own * own)
    for group in range(groups):
        head = summed_parts(ssum_ref, 16 * group, 8, 2, 8)
        tail = summed_parts(ssum_ref, 16 * groups + 16 * (group // 8) + group % 8, 1, 2, 8)
        for half in range(2):
            lanes = slice(half * LANES, (half + 1) * LANES)
            store_five(out_ref, 2 * group + half, head[:, lanes], tail[:, lanes], partial)


def owner_sums(values, ids, cameras):
    groups = cameras // 256
    tiles = []
    for value in values:
        parts = wide_parts(value, 2)
        tiles.append(jnp.concatenate(parts, axis=0).astype(BF16))
    rows = []
    for number in range(groups):
        hit = jnp.where(jnp.broadcast_to(ids >> 8, tiles[0].shape) == number, 1.0, 0.0).astype(BF16)
        rows += [tile * hit for tile in tiles]
    sums = contract(jnp.concatenate(rows, axis=0), one_hot_rows(ids & 255, 256))
    results = []
    height = values[0].shape[0]
    each = 2 * height * len(tiles)
    for place in range(len(values)):
        blocks = []
        for group in range(groups):
            start = group * each + place * 2 * height
            blocks.append(sums[start:start + height] + sums[start + height:start + 2 * height])
        results.append(jnp.concatenate(blocks, axis=1)[0:9])
    return results


def send_wanted(out_ref, precond, ids, scalar):
    cameras = precond.shape[1]
    for pair in range(out_ref.shape[0] // 10):
        own = ids[:, pair * LANES:(pair + 1) * LANES]
        low = jnp.broadcast_to(own & (LANES - 1), (8, LANES))
        high = jnp.broadcast_to(own >> 7, (8, LANES))
        head = jnp.zeros((8, LANES), F32)
        tail = jnp.zeros((8, LANES), F32)
        for block in range(cameras // LANES):
            lanes = slice(block * LANES, (block + 1) * LANES)
            hit = high == block
            head = jnp.where(hit, take_lanes(precond[0:8, lanes], low), head)
            last = jnp.broadcast_to(precond[8:9, lanes], (8, LANES))
            tail = jnp.where(hit, take_lanes(last, low), tail)
        store_five(out_ref, pair, head, tail[0:1], scalar)


def owner_start_kernel(in_ref, damp_ref, out_ref, residual_ref, scaling_ref, precond_ref, ids_ref):
    rhs, diag, ids = [], [], []
    left = left_half(9)
    for pair in range(in_ref.shape[0] // 20):
        even = in_ref[20 * pair:20 * pair + 9]
        odd = in_ref[20 * pair + 10:20 * pair + 19]
        low = jnp.where(left, even, swap_halves(odd))
        high = jnp.where(left, swap_halves(even), odd)
        pad = jnp.zeros((7, LANES), F32)
        rhs.append(jnp.concatenate([low, pad], axis=0))
        diag.append(jnp.concatenate([high, pad], axis=0))
        even = in_ref[20 * pair + 9:20 * pair + 10]
        odd = in_ref[20 * pair + 19:20 * pair + 20]
        ids.append(jnp.where(left_half(1), even, swap_halves(odd)).astype(jnp.int32))
    ids = jnp.concatenate(ids, axis=1)
    ids_ref[...] = ids
    rhs = jnp.concatenate(rhs, axis=1)
    diag = jnp.concatenate(diag, axis=1)
    residual, diag = owner_sums([rhs, diag], ids, damp_ref.shape[1])
    scaling = diag + damp_ref[...]
    precond = residual / scaling
    residual_ref[...] = residual
    scaling_ref[...] = scaling
    precond_ref[...] = precond
    send_wanted(out_ref, precond, ids, sum_all(residual * precond))


def owner_image(in_ref, ids, cameras):
    image = []
    pad = jnp.zeros((7, LANES), F32)
    for pair in range(in_ref.shape[0] // 10):
        head, tail = load_five(in_ref, pair)
        image.append(jnp.concatenate([head, tail, pad], axis=0))
    return owner_sums([jnp.concatenate(image, axis=1)], ids, cameras)[0]


def owner_middle_kernel(in_ref, ids_ref, rz_ref, damp_ref, direction_ref, residual_ref, scaling_ref,
                        out_ref, update_ref, newres_ref, precond_ref):
    ids = ids_ref[...]
    direction = direction_ref[...]
    image = owner_image(in_ref, ids, damp_ref.shape[1]) + damp_ref[...] * direction
    step = rz_ref[0:1, 0:1] / carried_scalar(in_ref)
    update_ref[...] = step * direction
    residual = residual_ref[...] - step * image
    precond = residual / scaling_ref[...]
    newres_ref[...] = residual
    precond_ref[...] = precond
    send_wanted(out_ref, precond, ids, sum_all(residual * precond))


def owner_end_kernel(in_ref, ids_ref, rz_ref, damp_ref, direction_ref, residual_ref, update_ref,
                     newupdate_ref, newres_ref):
    direction = direction_ref[...]
    image = owner_image(in_ref, ids_ref[...], damp_ref.shape[1]) + damp_ref[...] * direction
    step = rz_ref[0:1, 0:1] / carried_scalar(in_ref)
    newupdate_ref[...] = update_ref[...] + step * direction
    newres_ref[...] = residual_ref[...] - step * image


def call(kernel, outs, scratch, *args, smem=0, hbm=0):
    whole = pl.BlockSpec(memory_space=pltpu.VMEM)
    specs = [pl.BlockSpec(memory_space=pltpu.SMEM)] * smem + [pl.BlockSpec(memory_space=pltpu.HBM)] * hbm
    specs += [whole] * (len(args) - smem - hbm)
    return pl.pallas_call(
        kernel,
        out_shape=[jax.ShapeDtypeStruct(shape, dtype) for shape, dtype in outs],
        in_specs=specs,
        out_specs=[whole] * len(outs),
        scratch_shapes=scratch,
        compiler_params=pltpu.CompilerParams(vmem_limit_bytes=VMEM_BYTES),
    )(*args)


def exchange(blocks, shards):
    moved = lax.all_to_all(blocks.reshape(shards, 1, -1), AXES, split_axis=0, concat_axis=0, tiled=True)
    return moved.reshape(blocks.shape)


def start_call(chunk, *args):
    _, jac_cam, _, _, _, _, request, _ = args
    nobs = jac_cam.shape[1]
    shards = request.shape[0]
    groups = shards * CAP // 256
    copied = args[1:]
    scratch = [pltpu.VMEM((224, LANES), F32), pltpu.VMEM((groups * 32 + (groups + 7) // 8 * 32, 256), F32),
               pltpu.VMEM((3, 8, LANES), F32)]
    scratch += [pltpu.VMEM(arg.shape, arg.dtype) for arg in copied]
    scratch += [pltpu.SemaphoreType.DMA] * len(copied)
    outs = [((shards * 10, LANES), F32), ((32, nobs), F32), ((8, nobs), F32), ((8, nobs), F32),
            ((8, nobs), jnp.int32), ((6, 8, LANES), F32)]
    return call(functools.partial(start_kernel, chunk), outs, scratch, *args, smem=1, hbm=len(copied))


def apply_call(chunk, first, *args):
    arrived, camp = args[:2]
    nobs = camp.shape[1]
    shards = arrived.shape[0] // 5
    pairs = shards // 2
    groups = shards // 4
    cameras = args[6].shape[1]
    scratch = [pltpu.VMEM((80, LANES), F32), pltpu.VMEM((groups * 16 + (groups + 7) // 8 * 16, 256), F32),
               pltpu.VMEM((3, 8, LANES), F32), pltpu.VMEM((8, nobs), F32)]
    table = (pairs, 8, LANES)
    last = ((pairs + 7) // 8 * 8, LANES)
    scalar = ((8, LANES), F32)
    sent = ((shards * 5, LANES), F32)
    if first:
        outs = [sent, (table, F32), (last, F32), scalar]
    else:
        outs = [sent, ((9, cameras), F32), scalar]
        scratch += [pltpu.VMEM(table, F32), pltpu.VMEM(last, F32)]
    return call(functools.partial(apply_kernel, chunk, first), outs, scratch, *args)


def body(jac_cam, jac_pt, obs_residual, obs_point, obs_slot, request, obs_count, cam_damp, pt_damp):
    nobs = jac_cam.shape[1]
    shards = request.shape[0]
    cameras = cam_damp.shape[1]
    slots = shards * CAP
    chunk = 4096
    own = ((9, cameras), F32)
    sent = ((shards * 5, LANES), F32)
    sums, camp, pta, ptb, index, inverse = start_call(
        chunk, obs_count, jac_cam, jac_pt, obs_residual, obs_point.reshape(1, nobs), obs_slot.reshape(1, nobs),
        request, pt_damp.reshape(8, LANES))
    arrived = exchange(sums, shards)
    send, residual, scaling, precond, ids = call(
        owner_start_kernel, [sent, own, own, own, ((1, slots), jnp.int32)], [], arrived, cam_damp)
    arrived = exchange(send, shards)
    send, table, last, rz = apply_call(
        chunk, True, arrived, camp, pta, ptb, index, inverse, cam_damp, precond)
    arrived = exchange(send, shards)
    direction = precond
    send, update, residual, precond = call(
        owner_middle_kernel, [sent, own, own, own], [],
        arrived, ids, rz, cam_damp, direction, residual, scaling)
    arrived = exchange(send, shards)
    send, direction, rz = apply_call(
        chunk, False, arrived, camp, pta, ptb, index, inverse, cam_damp, precond, table, last, rz, direction)
    arrived = exchange(send, shards)
    update, residual = call(
        owner_end_kernel, [own, own], [], arrived, ids, rz, cam_damp, direction, residual, update)
    return update, residual


def solution(mesh):
    wide = P(None, AXES)
    flat = P(AXES)
    return jax.shard_map(
        body,
        mesh=mesh,
        in_specs=(wide, wide, wide, flat, flat, P(AXES, None), flat, wide, flat),
        out_specs=(wide, wide),
        check_vma=False,
    )
```

```python
import functools

import jax
import jax.numpy as jnp
from jax import lax
from jax.experimental import pallas as pl
from jax.experimental.pallas import tpu as pltpu
from jax.sharding import PartitionSpec as P

AXES = ("cell", "img")
F32 = jnp.float32
BF16 = jnp.bfloat16
LANES = 128
CAP = 64
VMEM_BYTES = 48 * 1024 * 1024


def iota(shape, dim):
    return lax.broadcasted_iota(jnp.int32, shape, dim)


def take_lanes(table, lanes):
    return jnp.take_along_axis(table, lanes, axis=1, mode="promise_in_bounds")


def contract(left, right):
    return lax.dot_general(left, right, (((1,), (1,)), ((), ())), preferred_element_type=F32)


def one_hot_rows(index, rows):
    hit = iota((rows, index.shape[1]), 0) == index
    return jnp.where(hit, 1.0, 0.0).astype(BF16)


def rounded_parts(value, count):
    parts = []
    for _ in range(count):
        part = value.astype(BF16)
        parts.append(part)
        value = value - part.astype(F32)
    return parts


def masked_rows(rows, hit):
    return [jnp.where(hit, jnp.broadcast_to(row, hit.shape), 0.0) for row in rows]


def stack_tiles(blocks):
    if len(blocks) % 2:
        blocks = blocks + [jnp.zeros_like(blocks[0])]
    return jnp.concatenate(blocks, axis=0).astype(BF16)


def group_hits(group):
    return jnp.broadcast_to(group, (8, group.shape[1])) == iota((8, group.shape[1]), 0)


def spread_slots(heads, tails, group, groups):
    width = group.shape[1]
    tiles = [jnp.concatenate(parts, axis=0).astype(BF16) for parts in heads]
    rows = []
    wide = jnp.broadcast_to(group, (8, width))
    for number in range(groups):
        hit = jnp.where(wide == number, 1.0, 0.0)
        hit = jnp.concatenate([hit, hit], axis=0).astype(BF16)
        rows += [tile * hit for tile in tiles]
    last = []
    for base in range(0, groups, 8):
        hit = wide == iota((8, width), 0) + base
        last += masked_rows(tails, hit)
    return jnp.concatenate(rows + [stack_tiles(last)], axis=0)


def wide_parts(value, count):
    return [part.astype(F32) for part in rounded_parts(value, count)]


def swap_halves(value):
    return pltpu.roll(value, CAP, 1)


def left_half(rows=8):
    return iota((rows, LANES), 1) < CAP


def sum_all(value):
    return jnp.sum(jnp.sum(value, axis=1, keepdims=True), axis=0, keepdims=True)


def carried_scalar(ref):
    total = ref[4:5, :]
    for sender in range(1, ref.shape[0] // 5):
        total = total + ref[5 * sender + 4:5 * sender + 5, :]
    return total[:, CAP:CAP + 1]


def store_five(out_ref, pair, head, tail, scalar):
    left = left_half()
    turned = swap_halves(head)
    even = jnp.where(left, head, pltpu.roll(turned, 4, 0))
    odd = jnp.where(left, turned, pltpu.roll(head, 4, 0))
    last = jnp.broadcast_to(tail, (8, LANES))
    last_even = jnp.where(left, last, scalar)
    last_odd = jnp.where(left, swap_halves(last), scalar)
    out_ref[10 * pair:10 * pair + 4] = even[0:4]
    out_ref[10 * pair + 4:10 * pair + 5] = last_even[0:1]
    out_ref[10 * pair + 5:10 * pair + 9] = odd[0:4]
    out_ref[10 * pair + 9:10 * pair + 10] = last_odd[0:1]


def load_five(in_ref, pair):
    left = left_half(4)
    even = in_ref[10 * pair:10 * pair + 4]
    odd = in_ref[10 * pair + 5:10 * pair + 9]
    low = jnp.where(left, even, swap_halves(odd))
    high = jnp.where(left, swap_halves(even), odd)
    last_even = in_ref[10 * pair + 4:10 * pair + 5]
    last_odd = in_ref[10 * pair + 9:10 * pair + 10]
    tail = jnp.where(left_half(1), last_even, swap_halves(last_odd))
    return jnp.concatenate([low, high], axis=0), tail


def point_spread(solved_ref, low, group, jac_a, jac_b):
    low = jnp.broadcast_to(low, (8, LANES))
    hit = group_hits(group)
    first = jnp.zeros((8, LANES), F32)
    second = jnp.zeros((8, LANES), F32)
    for axis in range(3):
        taken = jnp.where(hit, take_lanes(solved_ref[axis], low), 0.0)
        first = first + jac_a[axis:axis + 1] * taken
        second = second + jac_b[axis:axis + 1] * taken
    return jnp.sum(first, axis=0, keepdims=True), jnp.sum(second, axis=0, keepdims=True)


def solve_points(inverse_ref, totals, solved_ref):
    rows = ((0, 3, 5), (3, 1, 4), (5, 4, 2))
    for axis in range(3):
        solved_ref[axis] = (
            inverse_ref[rows[axis][0]] * totals[0]
            + inverse_ref[rows[axis][1]] * totals[1]
            + inverse_ref[rows[axis][2]] * totals[2]
        )


def summed_parts(sums_ref, start, rows, count, step):
    total = sums_ref[start:start + rows, :]
    for part in range(1, count):
        begin = start + part * step
        total = total + sums_ref[begin:begin + rows, :]
    return total


def start_kernel(chunk, count_ref, cam_hbm, pt_hbm, err_hbm, point_hbm, slot_hbm, req_hbm, damp_hbm,
                 out_ref, camp_ref, pta_ref, ptb_ref, index_ref, inverse_ref,
                 psum_ref, ssum_ref, solved_ref, cam_ref, pt_ref, err_ref, point_ref, slot_ref, req_ref, damp_ref,
                 cam_sem, pt_sem, err_sem, point_sem, slot_sem, req_sem, damp_sem):
    nobs = cam_ref.shape[1]
    copies = [
        pltpu.make_async_copy(pt_hbm, pt_ref, pt_sem),
        pltpu.make_async_copy(err_hbm, err_ref, err_sem),
        pltpu.make_async_copy(point_hbm, point_ref, point_sem),
        pltpu.make_async_copy(slot_hbm, slot_ref, slot_sem),
        pltpu.make_async_copy(damp_hbm, damp_ref, damp_sem),
        pltpu.make_async_copy(cam_hbm, cam_ref, cam_sem),
        pltpu.make_async_copy(req_hbm, req_ref, req_sem),
    ]
    for copy in copies:
        copy.start()
    count = count_ref[0]
    psum_ref[...] = jnp.zeros_like(psum_ref)
    ssum_ref[...] = jnp.zeros_like(ssum_ref)
    groups = req_ref.shape[0] * CAP // 256
    for copy in copies[:5]:
        copy.wait()

    def gather_points(step, carry):
        start = pl.multiple_of(step * chunk, chunk)
        lanes = pl.ds(start, chunk)
        live = iota((1, chunk), 1) + start < count
        point = point_ref[:, lanes]
        low = point & (LANES - 1)
        group = jnp.where(live, point >> 7, -1)
        slot = slot_ref[:, lanes]
        index_ref[0:1, lanes] = low
        index_ref[1:2, lanes] = group
        index_ref[2:3, lanes] = slot
        index_ref[3:4, lanes] = jnp.where(live, slot >> 8, -1)
        jac = pt_ref[:, lanes]
        zero = jnp.zeros((1, chunk), F32)
        jac_a = jnp.concatenate([jac[0:3], zero, jac[0:3], zero], axis=0)
        jac_b = jnp.concatenate([jac[3:6], zero, jac[3:6], zero], axis=0)
        pta_ref[:, lanes] = jac_a
        ptb_ref[:, lanes] = jac_b
        turn_a = jnp.concatenate([jac[0:3], zero, jac[1:3], jac[0:1], zero], axis=0)
        turn_b = jnp.concatenate([jac[3:6], zero, jac[4:6], jac[3:4], zero], axis=0)
        err = err_ref[:, lanes]
        blocks = wide_parts(jac_a * turn_a + jac_b * turn_b, 3)
        sides = wide_parts(jac_a * err[0:1] + jac_b * err[1:2], 3)
        rows = [block[place:place + 1] for block in blocks for place in (0, 1, 2, 4, 5, 6)]
        rows += [side[place:place + 1] for side in sides for place in (0, 1, 2)]
        spread = stack_tiles(masked_rows(rows, group_hits(group)))
        psum_ref[...] += contract(spread, one_hot_rows(low, LANES))
        return carry

    lax.fori_loop(0, nobs // chunk, gather_points, 0)

    damp = damp_ref[...]
    m00, m11, m22, m01, m12, m20 = [summed_parts(psum_ref, 8 * place, 8, 3, 48) for place in range(6)]
    m00, m11, m22 = m00 + damp, m11 + damp, m22 + damp
    c00 = m11 * m22 - m12 * m12
    c01 = m12 * m20 - m01 * m22
    c02 = m01 * m12 - m11 * m20
    c11 = m22 * m00 - m20 * m20
    c12 = m20 * m01 - m12 * m00
    c22 = m00 * m11 - m01 * m01
    det = m00 * c00 + m01 * c01 + m20 * c02
    for place, cofactor in enumerate((c00, c11, c22, c01, c12, c02)):
        inverse_ref[place] = cofactor / det
    solve_points(inverse_ref, [summed_parts(psum_ref, 144 + 8 * place, 8, 3, 24) for place in range(3)], solved_ref)
    for copy in copies[5:]:
        copy.wait()

    def scatter_terms(step, carry):
        start = pl.multiple_of(step * chunk, chunk)
        lanes = pl.ds(start, chunk)
        camp_ref[0:9, lanes] = cam_ref[0:9, lanes]
        camp_ref[9:16, lanes] = jnp.zeros((7, chunk), F32)
        camp_ref[16:25, lanes] = cam_ref[9:18, lanes]
        camp_ref[25:32, lanes] = jnp.zeros((7, chunk), F32)
        kept_a, kept_b = [], []
        for tile in range(chunk // LANES):
            spot = pl.ds(start + tile * LANES, LANES)
            first, second = point_spread(
                solved_ref, index_ref[0:1, spot], index_ref[1:2, spot], pta_ref[:, spot], ptb_ref[:, spot])
            err = err_ref[:, spot]
            kept_a.append(err[0:1] - first)
            kept_b.append(err[1:2] - second)
        kept_a = jnp.concatenate(kept_a, axis=1)
        kept_b = jnp.concatenate(kept_b, axis=1)
        cam_a = camp_ref[0:16, lanes]
        cam_b = camp_ref[16:32, lanes]
        rhs = wide_parts(-(cam_a * kept_a + cam_b * kept_b), 2)
        diag = wide_parts(cam_a * cam_a + cam_b * cam_b, 2)
        heads = [[part[0:8] for part in rhs], [part[0:8] for part in diag]]
        tails = [part[8:9] for part in rhs + diag]
        slot = index_ref[2:3, lanes]
        spread = spread_slots(heads, tails, index_ref[3:4, lanes], groups)
        ssum_ref[...] += contract(spread, one_hot_rows(slot & 255, 256))
        return carry

    lax.fori_loop(0, nobs // chunk, scatter_terms, 0)
    wanted = req_ref[...].astype(F32)
    wanted = jnp.concatenate([wanted, jnp.zeros_like(wanted)], axis=1)
    left = left_half()
    for group in range(groups):
        rhs = summed_parts(ssum_ref, 32 * group, 8, 2, 8)
        diag = summed_parts(ssum_ref, 32 * group + 16, 8, 2, 8)
        last = 32 * groups + 32 * (group // 8) + group % 8
        rhs_last = summed_parts(ssum_ref, last, 1, 2, 8)
        diag_last = summed_parts(ssum_ref, last + 16, 1, 2, 8)
        for half in range(2):
            lanes = slice(half * LANES, (half + 1) * LANES)
            row = 20 * (2 * group + half)
            out_ref[row:row + 8] = jnp.where(left, rhs[:, lanes], swap_halves(diag[:, lanes]))
            out_ref[row + 10:row + 18] = jnp.where(left, swap_halves(rhs[:, lanes]), diag[:, lanes])
            left_one = left_half(1)
            out_ref[row + 8:row + 9] = jnp.where(left_one, rhs_last[:, lanes], swap_halves(diag_last[:, lanes]))
            out_ref[row + 18:row + 19] = jnp.where(left_one, swap_halves(rhs_last[:, lanes]), diag_last[:, lanes])
            owner = 4 * group + 2 * half
            out_ref[row + 9:row + 10] = wanted[owner:owner + 1]
            out_ref[row + 19:row + 20] = wanted[owner + 1:owner + 2]


def apply_kernel(chunk, first, *refs):
    if first:
        (in_ref, camp_ref, pta_ref, ptb_ref, index_ref, inverse_ref, damp_ref, precond_ref,
         out_ref, table_ref, last_ref, rz_ref, psum_ref, ssum_ref, solved_ref, along_ref) = refs
    else:
        (in_ref, camp_ref, pta_ref, ptb_ref, index_ref, inverse_ref, damp_ref, precond_ref,
         oldtable_ref, oldlast_ref, oldrz_ref, oldown_ref,
         out_ref, own_ref, rz_ref, psum_ref, ssum_ref, solved_ref, along_ref, table_ref, last_ref) = refs
    nobs = camp_ref.shape[1]
    psum_ref[...] = jnp.zeros_like(psum_ref)
    ssum_ref[...] = jnp.zeros_like(ssum_ref)
    pairs = table_ref.shape[0]
    groups = pairs // 2
    rz = carried_scalar(in_ref)
    rz_ref[...] = jnp.broadcast_to(rz, rz_ref.shape)
    own = precond_ref[...]
    if not first:
        beta = rz / oldrz_ref[0:1, 0:1]
        own = own + beta * oldown_ref[...]
        own_ref[...] = own
    for pair in range(pairs):
        head, tail = load_five(in_ref, pair)
        if not first:
            head = head + beta * oldtable_ref[pair]
            tail = tail + beta * oldlast_ref[pair:pair + 1]
        table_ref[pair] = head
        last_ref[pair:pair + 1] = tail

    def gather_points(step, carry):
        start = pl.multiple_of(step * chunk, chunk)
        lanes = pl.ds(start, chunk)
        for tile in range(chunk // LANES):
            spot = pl.ds(start + tile * LANES, LANES)
            slot = index_ref[2:3, spot]
            low = jnp.broadcast_to(slot & (LANES - 1), (8, LANES))
            high = jnp.broadcast_to(slot >> 7, (8, LANES))
            taken = jnp.zeros((8, LANES), F32)
            for pair in range(pairs):
                taken = jnp.where(high == pair, take_lanes(table_ref[pair], low), taken)
            tail = jnp.zeros((8, LANES), F32)
            for base in range(0, pairs, 8):
                hit = high == iota((8, LANES), 0) + base
                tail = jnp.where(hit, take_lanes(last_ref[base:base + 8], low), tail)
            tail = jnp.sum(tail, axis=0, keepdims=True)
            along_ref[0:1, spot] = jnp.sum(camp_ref[0:8, spot] * taken, axis=0, keepdims=True) + camp_ref[8:9, spot] * tail
            along_ref[1:2, spot] = jnp.sum(camp_ref[16:24, spot] * taken, axis=0, keepdims=True) + camp_ref[24:25, spot] * tail
        sides = wide_parts(pta_ref[:, lanes] * along_ref[0:1, lanes] + ptb_ref[:, lanes] * along_ref[1:2, lanes], 3)
        rows = [side[place:place + 1] for side in sides for place in (0, 1, 2)]
        spread = stack_tiles(masked_rows(rows, group_hits(index_ref[1:2, lanes])))
        psum_ref[...] += contract(spread, one_hot_rows(index_ref[0:1, lanes], LANES))
        return carry

    lax.fori_loop(0, nobs // chunk, gather_points, 0)
    solve_points(inverse_ref, [summed_parts(psum_ref, 8 * place, 8, 3, 24) for place in range(3)], solved_ref)

    def scatter_terms(step, carry):
        start = pl.multiple_of(step * chunk, chunk)
        lanes = pl.ds(start, chunk)
        kept_a, kept_b = [], []
        for tile in range(chunk // LANES):
            spot = pl.ds(start + tile * LANES, LANES)
            first_sum, second_sum = point_spread(
                solved_ref, index_ref[0:1, spot], index_ref[1:2, spot], pta_ref[:, spot], ptb_ref[:, spot])
            kept_a.append(along_ref[0:1, spot] - first_sum)
            kept_b.append(along_ref[1:2, spot] - second_sum)
        kept_a = jnp.concatenate(kept_a, axis=1)
        kept_b = jnp.concatenate(kept_b, axis=1)
        terms = wide_parts(camp_ref[0:16, lanes] * kept_a + camp_ref[16:32, lanes] * kept_b, 2)
        group = index_ref[3:4, lanes]
        spread = spread_slots([[part[0:8] for part in terms]], [part[8:9] for part in terms], group, groups)
        ssum_ref[...] += contract(spread, one_hot_rows(index_ref[2:3, lanes] & 255, 256))
        energy = along_ref[0:1, lanes] * kept_a + along_ref[1:2, lanes] * kept_b
        return carry + jnp.where(group >= 0, energy, 0.0)

    energy = lax.fori_loop(0, nobs // chunk, scatter_terms, jnp.zeros((1, chunk), F32))
    partial = sum_all(energy) + sum_all(damp_ref[...] * own * own)
    for group in range(groups):
        head = summed_parts(ssum_ref, 16 * group, 8, 2, 8)
        tail = summed_parts(ssum_ref, 16 * groups + 16 * (group // 8) + group % 8, 1, 2, 8)
        for half in range(2):
            lanes = slice(half * LANES, (half + 1) * LANES)
            store_five(out_ref, 2 * group + half, head[:, lanes], tail[:, lanes], partial)


def owner_sums(values, ids, cameras):
    groups = cameras // 256
    tiles = []
    for value in values:
        parts = wide_parts(value, 2)
        tiles.append(jnp.concatenate(parts, axis=0).astype(BF16))
    rows = []
    for number in range(groups):
        hit = jnp.where(jnp.broadcast_to(ids >> 8, tiles[0].shape) == number, 1.0, 0.0).astype(BF16)
        rows += [tile * hit for tile in tiles]
    sums = contract(jnp.concatenate(rows, axis=0), one_hot_rows(ids & 255, 256))
    results = []
    height = values[0].shape[0]
    each = 2 * height * len(tiles)
    for place in range(len(values)):
        blocks = []
        for group in range(groups):
            start = group * each + place * 2 * height
            blocks.append(sums[start:start + height] + sums[start + height:start + 2 * height])
        results.append(jnp.concatenate(blocks, axis=1)[0:9])
    return results


def send_wanted(out_ref, precond, ids, scalar):
    cameras = precond.shape[1]
    for pair in range(out_ref.shape[0] // 10):
        own = ids[:, pair * LANES:(pair + 1) * LANES]
        low = jnp.broadcast_to(own & (LANES - 1), (8, LANES))
        high = jnp.broadcast_to(own >> 7, (8, LANES))
        head = jnp.zeros((8, LANES), F32)
        tail = jnp.zeros((8, LANES), F32)
        for block in range(cameras // LANES):
            lanes = slice(block * LANES, (block + 1) * LANES)
            hit = high == block
            head = jnp.where(hit, take_lanes(precond[0:8, lanes], low), head)
            last = jnp.broadcast_to(precond[8:9, lanes], (8, LANES))
            tail = jnp.where(hit, take_lanes(last, low), tail)
        store_five(out_ref, pair, head, tail[0:1], scalar)


def owner_start_kernel(in_ref, damp_ref, out_ref, residual_ref, scaling_ref, precond_ref, ids_ref):
    rhs, diag, ids = [], [], []
    left = left_half(9)
    for pair in range(in_ref.shape[0] // 20):
        even = in_ref[20 * pair:20 * pair + 9]
        odd = in_ref[20 * pair + 10:20 * pair + 19]
        low = jnp.where(left, even, swap_halves(odd))
        high = jnp.where(left, swap_halves(even), odd)
        pad = jnp.zeros((7, LANES), F32)
        rhs.append(jnp.concatenate([low, pad], axis=0))
        diag.append(jnp.concatenate([high, pad], axis=0))
        even = in_ref[20 * pair + 9:20 * pair + 10]
        odd = in_ref[20 * pair + 19:20 * pair + 20]
        ids.append(jnp.where(left_half(1), even, swap_halves(odd)).astype(jnp.int32))
    ids = jnp.concatenate(ids, axis=1)
    ids_ref[...] = ids
    rhs = jnp.concatenate(rhs, axis=1)
    diag = jnp.concatenate(diag, axis=1)
    residual, diag = owner_sums([rhs, diag], ids, damp_ref.shape[1])
    scaling = diag + damp_ref[...]
    precond = residual / scaling
    residual_ref[...] = residual
    scaling_ref[...] = scaling
    precond_ref[...] = precond
    send_wanted(out_ref, precond, ids, sum_all(residual * precond))


def owner_image(in_ref, ids, cameras):
    image = []
    pad = jnp.zeros((7, LANES), F32)
    for pair in range(in_ref.shape[0] // 10):
        head, tail = load_five(in_ref, pair)
        image.append(jnp.concatenate([head, tail, pad], axis=0))
    return owner_sums([jnp.concatenate(image, axis=1)], ids, cameras)[0]


def owner_middle_kernel(in_ref, ids_ref, rz_ref, damp_ref, direction_ref, residual_ref, scaling_ref,
                        out_ref, update_ref, newres_ref, precond_ref):
    ids = ids_ref[...]
    direction = direction_ref[...]
    image = owner_image(in_ref, ids, damp_ref.shape[1]) + damp_ref[...] * direction
    step = rz_ref[0:1, 0:1] / carried_scalar(in_ref)
    update_ref[...] = step * direction
    residual = residual_ref[...] - step * image
    precond = residual / scaling_ref[...]
    newres_ref[...] = residual
    precond_ref[...] = precond
    send_wanted(out_ref, precond, ids, sum_all(residual * precond))


def owner_end_kernel(in_ref, ids_ref, rz_ref, damp_ref, direction_ref, residual_ref, update_ref,
                     newupdate_ref, newres_ref):
    direction = direction_ref[...]
    image = owner_image(in_ref, ids_ref[...], damp_ref.shape[1]) + damp_ref[...] * direction
    step = rz_ref[0:1, 0:1] / carried_scalar(in_ref)
    newupdate_ref[...] = update_ref[...] + step * direction
    newres_ref[...] = residual_ref[...] - step * image


def call(kernel, outs, scratch, *args, smem=0, hbm=0):
    whole = pl.BlockSpec(memory_space=pltpu.VMEM)
    specs = [pl.BlockSpec(memory_space=pltpu.SMEM)] * smem + [pl.BlockSpec(memory_space=pltpu.HBM)] * hbm
    specs += [whole] * (len(args) - smem - hbm)
    return pl.pallas_call(
        kernel,
        out_shape=[jax.ShapeDtypeStruct(shape, dtype) for shape, dtype in outs],
        in_specs=specs,
        out_specs=[whole] * len(outs),
        scratch_shapes=scratch,
        compiler_params=pltpu.CompilerParams(vmem_limit_bytes=VMEM_BYTES),
    )(*args)


def exchange(blocks, shards):
    moved = lax.all_to_all(blocks.reshape(shards, 1, -1), AXES, split_axis=0, concat_axis=0, tiled=True)
    return moved.reshape(blocks.shape)


def start_call(chunk, *args):
    _, jac_cam, _, _, _, _, request, _ = args
    nobs = jac_cam.shape[1]
    shards = request.shape[0]
    groups = shards * CAP // 256
    copied = args[1:]
    scratch = [pltpu.VMEM((224, LANES), F32), pltpu.VMEM((groups * 32 + (groups + 7) // 8 * 32, 256), F32),
               pltpu.VMEM((3, 8, LANES), F32)]
    scratch += [pltpu.VMEM(arg.shape, arg.dtype) for arg in copied]
    scratch += [pltpu.SemaphoreType.DMA] * len(copied)
    outs = [((shards * 10, LANES), F32), ((32, nobs), F32), ((8, nobs), F32), ((8, nobs), F32),
            ((8, nobs), jnp.int32), ((6, 8, LANES), F32)]
    copied = [pltpu.with_memory_space_constraint(arg, pltpu.HBM) for arg in copied]
    return call(functools.partial(start_kernel, chunk), outs, scratch, args[0], *copied, smem=1, hbm=len(copied))


def apply_call(chunk, first, *args):
    arrived, camp = args[:2]
    nobs = camp.shape[1]
    shards = arrived.shape[0] // 5
    pairs = shards // 2
    groups = shards // 4
    cameras = args[6].shape[1]
    scratch = [pltpu.VMEM((80, LANES), F32), pltpu.VMEM((groups * 16 + (groups + 7) // 8 * 16, 256), F32),
               pltpu.VMEM((3, 8, LANES), F32), pltpu.VMEM((8, nobs), F32)]
    table = (pairs, 8, LANES)
    last = ((pairs + 7) // 8 * 8, LANES)
    scalar = ((8, LANES), F32)
    sent = ((shards * 5, LANES), F32)
    if first:
        outs = [sent, (table, F32), (last, F32), scalar]
    else:
        outs = [sent, ((9, cameras), F32), scalar]
        scratch += [pltpu.VMEM(table, F32), pltpu.VMEM(last, F32)]
    return call(functools.partial(apply_kernel, chunk, first), outs, scratch, *args)


def body(jac_cam, jac_pt, obs_residual, obs_point, obs_slot, request, obs_count, cam_damp, pt_damp):
    nobs = jac_cam.shape[1]
    shards = request.shape[0]
    cameras = cam_damp.shape[1]
    slots = shards * CAP
    chunk = 4096
    own = ((9, cameras), F32)
    sent = ((shards * 5, LANES), F32)
    sums, camp, pta, ptb, index, inverse = start_call(
        chunk, obs_count, jac_cam, jac_pt, obs_residual, obs_point.reshape(1, nobs), obs_slot.reshape(1, nobs),
        request, pt_damp.reshape(8, LANES))
    arrived = exchange(sums, shards)
    send, residual, scaling, precond, ids = call(
        owner_start_kernel, [sent, own, own, own, ((1, slots), jnp.int32)], [], arrived, cam_damp)
    arrived = exchange(send, shards)
    send, table, last, rz = apply_call(
        chunk, True, arrived, camp, pta, ptb, index, inverse, cam_damp, precond)
    arrived = exchange(send, shards)
    direction = precond
    send, update, residual, precond = call(
        owner_middle_kernel, [sent, own, own, own], [],
        arrived, ids, rz, cam_damp, direction, residual, scaling)
    arrived = exchange(send, shards)
    send, direction, rz = apply_call(
        chunk, False, arrived, camp, pta, ptb, index, inverse, cam_damp, precond, table, last, rz, direction)
    arrived = exchange(send, shards)
    update, residual = call(
        owner_end_kernel, [own, own], [], arrived, ids, rz, cam_damp, direction, residual, update)
    return update, residual


def solution(mesh):
    wide = P(None, AXES)
    flat = P(AXES)
    return jax.shard_map(
        body,
        mesh=mesh,
        in_specs=(wide, wide, wide, flat, flat, P(AXES, None), flat, wide, flat),
        out_specs=(wide, wide),
        check_vma=False,
    )
```

```python
import functools

import jax
import jax.numpy as jnp
from jax import lax
from jax.experimental import pallas as pl
from jax.experimental.pallas import tpu as pltpu
from jax.sharding import PartitionSpec as P

AXES = ("cell", "img")
F32 = jnp.float32
BF16 = jnp.bfloat16
LANES = 128
CAP = 64
VMEM_BYTES = 32 * 1024 * 1024


def iota(shape, dim):
    return lax.broadcasted_iota(jnp.int32, shape, dim)


def take_lanes(table, lanes):
    return jnp.take_along_axis(table, lanes, axis=1, mode="promise_in_bounds")


def contract(left, right):
    return lax.dot_general(left, right, (((1,), (1,)), ((), ())), preferred_element_type=F32)


def one_hot_rows(index, rows):
    hit = iota((rows, index.shape[1]), 0) == index
    return jnp.where(hit, 1.0, 0.0).astype(BF16)


def one_hot_columns(index, columns):
    spread = jnp.broadcast_to(index.astype(F32), (LANES, LANES)).astype(BF16).T
    spread = jnp.concatenate([spread] * (columns // LANES), axis=1)
    lane = iota((LANES, columns), 1).astype(F32).astype(BF16)
    return jnp.where(spread == lane, jnp.ones((), BF16), jnp.zeros((), BF16))


def rounded_parts(value, count):
    parts = []
    for _ in range(count):
        part = value.astype(BF16)
        parts.append(part)
        value = value - part.astype(F32)
    return parts


def masked_rows(rows, hit):
    return [jnp.where(hit, jnp.broadcast_to(row, hit.shape), 0.0) for row in rows]


def stack_tiles(blocks):
    if len(blocks) % 2:
        blocks = blocks + [jnp.zeros_like(blocks[0])]
    return jnp.concatenate(blocks, axis=0).astype(BF16)


def group_hits(group):
    return jnp.broadcast_to(group, (8, group.shape[1])) == iota((8, group.shape[1]), 0)


def spread_slots(heads, tails, group, groups):
    width = group.shape[1]
    tiles = [jnp.concatenate(parts, axis=0).astype(BF16) for parts in heads]
    rows = []
    wide = jnp.broadcast_to(group, (8, width))
    for number in range(groups):
        hit = jnp.where(wide == number, 1.0, 0.0)
        hit = jnp.concatenate([hit, hit], axis=0).astype(BF16)
        rows += [tile * hit for tile in tiles]
    last = []
    for base in range(0, groups, 8):
        hit = wide == iota((8, width), 0) + base
        last += masked_rows(tails, hit)
    return jnp.concatenate(rows + [stack_tiles(last)], axis=0)


def wide_parts(value, count):
    return [part.astype(F32) for part in rounded_parts(value, count)]


def swap_halves(value):
    return pltpu.roll(value, CAP, 1)


def left_half(rows=8):
    return iota((rows, LANES), 1) < CAP


def sum_all(value):
    return jnp.sum(jnp.sum(value, axis=1, keepdims=True), axis=0, keepdims=True)


def carried_scalar(ref):
    total = ref[4:5, :]
    for sender in range(1, ref.shape[0] // 5):
        total = total + ref[5 * sender + 4:5 * sender + 5, :]
    return total[:, CAP:CAP + 1]


def store_five(out_ref, pair, head, tail, scalar):
    left = left_half()
    turned = swap_halves(head)
    even = jnp.where(left, head, pltpu.roll(turned, 4, 0))
    odd = jnp.where(left, turned, pltpu.roll(head, 4, 0))
    last = jnp.broadcast_to(tail, (8, LANES))
    last_even = jnp.where(left, last, scalar)
    last_odd = jnp.where(left, swap_halves(last), scalar)
    out_ref[10 * pair:10 * pair + 4] = even[0:4]
    out_ref[10 * pair + 4:10 * pair + 5] = last_even[0:1]
    out_ref[10 * pair + 5:10 * pair + 9] = odd[0:4]
    out_ref[10 * pair + 9:10 * pair + 10] = last_odd[0:1]


def load_five(in_ref, pair):
    left = left_half(4)
    even = in_ref[10 * pair:10 * pair + 4]
    odd = in_ref[10 * pair + 5:10 * pair + 9]
    low = jnp.where(left, even, swap_halves(odd))
    high = jnp.where(left, swap_halves(even), odd)
    last_even = in_ref[10 * pair + 4:10 * pair + 5]
    last_odd = in_ref[10 * pair + 9:10 * pair + 10]
    tail = jnp.where(left_half(1), last_even, swap_halves(last_odd))
    return jnp.concatenate([low, high], axis=0), tail


def pipelined(steps, build, product):
    for step in range(steps):
        build(step)
        if step:
            product(step - 1)
    product(steps - 1)


def chunk_lanes(step, chunk):
    return slice(step * chunk, (step + 1) * chunk)


def add_product(sums_ref, left_ref, right_ref, lanes, first):
    product = jnp.dot(left_ref[:, lanes], right_ref[lanes, :], preferred_element_type=F32)
    if first:
        sums_ref[...] = product
    else:
        sums_ref[...] += product


def point_spread(solved_ref, low, group, jac):
    low = jnp.broadcast_to(low, (8, LANES))
    hit = group_hits(group)
    first = jnp.zeros((8, LANES), F32)
    second = jnp.zeros((8, LANES), F32)
    for axis in range(3):
        taken = jnp.where(hit, take_lanes(solved_ref[axis], low), 0.0)
        first = first + jac[axis:axis + 1] * taken
        second = second + jac[axis + 4:axis + 5] * taken
    return jnp.sum(first, axis=0, keepdims=True), jnp.sum(second, axis=0, keepdims=True)


def two_level(jac, first, second):
    both = jac * jnp.where(iota(jac.shape, 0) < 4, first, second)
    return both + pltpu.roll(both, 4, 0)


def kept_rows(solved_ref, index_ref, jac_ref, along_ref, start, chunk):
    kept_a, kept_b = [], []
    for tile in range(chunk // LANES):
        spot = slice(start + tile * LANES, start + (tile + 1) * LANES)
        first, second = point_spread(solved_ref, index_ref[0:1, spot], index_ref[1:2, spot], jac_ref[:, spot])
        kept_a.append(along_ref[0:1, spot] - first)
        kept_b.append(along_ref[1:2, spot] - second)
    return jnp.concatenate(kept_a, axis=1), jnp.concatenate(kept_b, axis=1)


def solve_points(inverse_ref, totals, solved_ref):
    rows = ((0, 3, 5), (3, 1, 4), (5, 4, 2))
    for axis in range(3):
        solved_ref[axis] = (
            inverse_ref[rows[axis][0]] * totals[0]
            + inverse_ref[rows[axis][1]] * totals[1]
            + inverse_ref[rows[axis][2]] * totals[2]
        )


def summed_parts(sums_ref, start, rows, count, step):
    total = sums_ref[start:start + rows, :]
    for part in range(1, count):
        begin = start + part * step
        total = total + sums_ref[begin:begin + rows, :]
    return total


def start_kernel(chunk, count_ref, cam_hbm, pt_hbm, err_hbm, point_hbm, slot_hbm, req_hbm, damp_hbm, camdamp_hbm,
                 out_ref, camp_ref, jac_ref, index_ref, pointhot_ref, slothot_ref, inverse_ref, camdamp_ref,
                 psum_ref, ssum_ref, solved_ref, pointrows_ref, slotrows_ref,
                 cam_ref, pt_ref, err_ref, point_ref, slot_ref, req_ref, damp_ref,
                 cam_sem, pt_sem, err_sem, point_sem, slot_sem, req_sem, damp_sem, camdamp_sem):
    nobs = cam_ref.shape[1]
    steps = nobs // chunk
    copies = [
        pltpu.make_async_copy(pt_hbm, pt_ref, pt_sem),
        pltpu.make_async_copy(err_hbm, err_ref, err_sem),
        pltpu.make_async_copy(point_hbm, point_ref, point_sem),
        pltpu.make_async_copy(slot_hbm, slot_ref, slot_sem),
        pltpu.make_async_copy(damp_hbm, damp_ref, damp_sem),
        pltpu.make_async_copy(cam_hbm, cam_ref, cam_sem),
        pltpu.make_async_copy(req_hbm, req_ref, req_sem),
        pltpu.make_async_copy(camdamp_hbm, camdamp_ref, camdamp_sem),
    ]
    for copy in copies:
        copy.start()
    count = count_ref[0]
    groups = req_ref.shape[0] * CAP // 256
    for copy in copies[:5]:
        copy.wait()

    def build_points(step):
        lanes = chunk_lanes(step, chunk)
        live = iota((1, chunk), 1) + step * chunk < count
        point = point_ref[:, lanes]
        low = point & (LANES - 1)
        group = jnp.where(live, point >> 7, -1)
        slot = slot_ref[:, lanes]
        index_ref[0:1, lanes] = low
        index_ref[1:2, lanes] = group
        index_ref[2:3, lanes] = slot
        index_ref[3:4, lanes] = jnp.where(live, slot >> 8, -1)
        for tile in range(chunk // LANES):
            spot = slice(step * chunk + tile * LANES, step * chunk + (tile + 1) * LANES)
            part = chunk_lanes(tile, LANES)
            pointhot_ref[spot, :] = one_hot_columns(low[:, part], LANES)
            slothot_ref[spot, :] = one_hot_columns(slot[:, part] & 255, 256)
        jac = pt_ref[:, lanes]
        zero = jnp.zeros((1, chunk), F32)
        jac_ref[:, lanes] = jnp.concatenate([jac[0:3], zero, jac[3:6], zero], axis=0)
        jac_a = jnp.concatenate([jac[0:3], zero, jac[0:3], zero], axis=0)
        jac_b = jnp.concatenate([jac[3:6], zero, jac[3:6], zero], axis=0)
        turn_a = jnp.concatenate([jac[0:3], zero, jac[1:3], jac[0:1], zero], axis=0)
        turn_b = jnp.concatenate([jac[3:6], zero, jac[4:6], jac[3:4], zero], axis=0)
        err = err_ref[:, lanes]
        blocks = wide_parts(jac_a * turn_a + jac_b * turn_b, 3)
        sides = wide_parts(jac_a * err[0:1] + jac_b * err[1:2], 3)
        rows = [block[place:place + 1] for block in blocks for place in (0, 1, 2, 4, 5, 6)]
        rows += [side[place:place + 1] for side in sides for place in (0, 1, 2)]
        pointrows_ref[:, lanes] = stack_tiles(masked_rows(rows, group_hits(group)))

    pipelined(steps, build_points, lambda step: add_product(
        psum_ref, pointrows_ref, pointhot_ref, chunk_lanes(step, chunk), step == 0))

    damp = damp_ref[...]
    m00, m11, m22, m01, m12, m20 = [summed_parts(psum_ref, 8 * place, 8, 3, 48) for place in range(6)]
    m00, m11, m22 = m00 + damp, m11 + damp, m22 + damp
    c00 = m11 * m22 - m12 * m12
    c01 = m12 * m20 - m01 * m22
    c02 = m01 * m12 - m11 * m20
    c11 = m22 * m00 - m20 * m20
    c12 = m20 * m01 - m12 * m00
    c22 = m00 * m11 - m01 * m01
    det = m00 * c00 + m01 * c01 + m20 * c02
    for place, cofactor in enumerate((c00, c11, c22, c01, c12, c02)):
        inverse_ref[place] = cofactor / det
    solve_points(inverse_ref, [summed_parts(psum_ref, 144 + 8 * place, 8, 3, 24) for place in range(3)], solved_ref)
    for copy in copies[5:]:
        copy.wait()

    def build_slots(step):
        lanes = chunk_lanes(step, chunk)
        cam_a = cam_ref[0:8, lanes]
        cam_b = cam_ref[9:17, lanes]
        last = jnp.concatenate([cam_ref[8:9, lanes], cam_ref[17:18, lanes], jnp.zeros((6, chunk), F32)], axis=0)
        camp_ref[0:8, lanes] = cam_a
        camp_ref[8:16, lanes] = cam_b
        camp_ref[16:24, lanes] = last
        kept_a, kept_b = kept_rows(solved_ref, index_ref, jac_ref, err_ref, step * chunk, chunk)
        rhs = wide_parts(-(cam_a * kept_a + cam_b * kept_b), 2)
        diag = wide_parts(cam_a * cam_a + cam_b * cam_b, 2)
        last_a, last_b = last[0:1], last[1:2]
        tails = wide_parts(-(last_a * kept_a + last_b * kept_b), 2) + wide_parts(last_a * last_a + last_b * last_b, 2)
        slotrows_ref[:, lanes] = spread_slots([rhs, diag], tails, index_ref[3:4, lanes], groups)

    pipelined(steps, build_slots, lambda step: add_product(
        ssum_ref, slotrows_ref, slothot_ref, chunk_lanes(step, chunk), step == 0))
    wanted = req_ref[...].astype(F32)
    wanted = jnp.concatenate([wanted, jnp.zeros_like(wanted)], axis=1)
    left = left_half()
    left_one = left_half(1)
    for group in range(groups):
        rhs = summed_parts(ssum_ref, 32 * group, 8, 2, 8)
        diag = summed_parts(ssum_ref, 32 * group + 16, 8, 2, 8)
        last = 32 * groups + 32 * (group // 8) + group % 8
        rhs_last = summed_parts(ssum_ref, last, 1, 2, 8)
        diag_last = summed_parts(ssum_ref, last + 16, 1, 2, 8)
        for half in range(2):
            lanes = slice(half * LANES, (half + 1) * LANES)
            row = 20 * (2 * group + half)
            out_ref[row:row + 8] = jnp.where(left, rhs[:, lanes], swap_halves(diag[:, lanes]))
            out_ref[row + 10:row + 18] = jnp.where(left, swap_halves(rhs[:, lanes]), diag[:, lanes])
            out_ref[row + 8:row + 9] = jnp.where(left_one, rhs_last[:, lanes], swap_halves(diag_last[:, lanes]))
            out_ref[row + 18:row + 19] = jnp.where(left_one, swap_halves(rhs_last[:, lanes]), diag_last[:, lanes])
            owner = 4 * group + 2 * half
            out_ref[row + 9:row + 10] = wanted[owner:owner + 1]
            out_ref[row + 19:row + 20] = wanted[owner + 1:owner + 2]


def apply_kernel(chunk, first, *refs):
    if first:
        (in_ref, camp_ref, jac_ref, index_ref, pointhot_ref, slothot_ref, inverse_ref, damp_ref, precond_ref,
         out_ref, table_ref, last_ref, rz_ref, *work) = refs
    else:
        (in_ref, camp_ref, jac_ref, index_ref, pointhot_ref, slothot_ref, inverse_ref, damp_ref, precond_ref,
         oldtable_ref, oldlast_ref, oldrz_ref, oldown_ref,
         out_ref, own_ref, rz_ref, *work, table_ref, last_ref) = refs
    psum_ref, ssum_ref, solved_ref, along_ref, pointrows_ref, slotrows_ref = work
    nobs = camp_ref.shape[1]
    steps = nobs // chunk
    pairs = table_ref.shape[0]
    groups = pairs // 2
    rz = carried_scalar(in_ref)
    rz_ref[...] = jnp.broadcast_to(rz, rz_ref.shape)
    own = precond_ref[...]
    if not first:
        beta = rz / oldrz_ref[0:1, 0:1]
        own = own + beta * oldown_ref[...]
        own_ref[...] = own
    for pair in range(pairs):
        head, tail = load_five(in_ref, pair)
        if not first:
            head = head + beta * oldtable_ref[pair]
            tail = tail + beta * oldlast_ref[pair:pair + 1]
        table_ref[pair] = head
        last_ref[pair:pair + 1] = tail

    def build_points(step):
        lanes = chunk_lanes(step, chunk)
        for tile in range(chunk // LANES):
            spot = slice(step * chunk + tile * LANES, step * chunk + (tile + 1) * LANES)
            slot = index_ref[2:3, spot]
            low = jnp.broadcast_to(slot & (LANES - 1), (8, LANES))
            high = jnp.broadcast_to(slot >> 7, (8, LANES))
            taken = jnp.zeros((8, LANES), F32)
            for pair in range(pairs):
                taken = jnp.where(high == pair, take_lanes(table_ref[pair], low), taken)
            tail = jnp.zeros((8, LANES), F32)
            for base in range(0, pairs, 8):
                hit = high == iota((8, LANES), 0) + base
                tail = jnp.where(hit, take_lanes(last_ref[base:base + 8], low), tail)
            tail = jnp.sum(tail, axis=0, keepdims=True)
            along_ref[0:1, spot] = jnp.sum(camp_ref[0:8, spot] * taken, axis=0, keepdims=True) + camp_ref[16:17, spot] * tail
            along_ref[1:2, spot] = jnp.sum(camp_ref[8:16, spot] * taken, axis=0, keepdims=True) + camp_ref[17:18, spot] * tail
        sides = wide_parts(two_level(jac_ref[:, lanes], along_ref[0:1, lanes], along_ref[1:2, lanes]), 3)
        rows = [side[place:place + 1] for side in sides for place in (0, 1, 2)]
        pointrows_ref[:, lanes] = stack_tiles(masked_rows(rows, group_hits(index_ref[1:2, lanes])))

    pipelined(steps, build_points, lambda step: add_product(
        psum_ref, pointrows_ref, pointhot_ref, chunk_lanes(step, chunk), step == 0))
    solve_points(inverse_ref, [summed_parts(psum_ref, 8 * place, 8, 3, 24) for place in range(3)], solved_ref)
    energies = []

    def build_slots(step):
        lanes = chunk_lanes(step, chunk)
        kept_a, kept_b = kept_rows(solved_ref, index_ref, jac_ref, along_ref, step * chunk, chunk)
        heads = wide_parts(camp_ref[0:8, lanes] * kept_a + camp_ref[8:16, lanes] * kept_b, 2)
        tails = wide_parts(camp_ref[16:17, lanes] * kept_a + camp_ref[17:18, lanes] * kept_b, 2)
        group = index_ref[3:4, lanes]
        slotrows_ref[:, lanes] = spread_slots([heads], tails, group, groups)
        energy = along_ref[0:1, lanes] * kept_a + along_ref[1:2, lanes] * kept_b
        energies.append(jnp.where(group >= 0, energy, 0.0))

    pipelined(steps, build_slots, lambda step: add_product(
        ssum_ref, slotrows_ref, slothot_ref, chunk_lanes(step, chunk), step == 0))
    energy = energies[0]
    for more in energies[1:]:
        energy = energy + more
    partial = sum_all(energy) + sum_all(damp_ref[...] * own * own)
    for group in range(groups):
        head = summed_parts(ssum_ref, 16 * group, 8, 2, 8)
        tail = summed_parts(ssum_ref, 16 * groups + 16 * (group // 8) + group % 8, 1, 2, 8)
        for half in range(2):
            lanes = slice(half * LANES, (half + 1) * LANES)
            store_five(out_ref, 2 * group + half, head[:, lanes], tail[:, lanes], partial)


def owner_sums(values, ids, cameras):
    groups = cameras // 256
    tiles = []
    for value in values:
        parts = wide_parts(value, 2)
        tiles.append(jnp.concatenate(parts, axis=0).astype(BF16))
    rows = []
    for number in range(groups):
        hit = jnp.where(jnp.broadcast_to(ids >> 8, tiles[0].shape) == number, 1.0, 0.0).astype(BF16)
        rows += [tile * hit for tile in tiles]
    sums = contract(jnp.concatenate(rows, axis=0), one_hot_rows(ids & 255, 256))
    results = []
    height = values[0].shape[0]
    each = 2 * height * len(tiles)
    for place in range(len(values)):
        blocks = []
        for group in range(groups):
            start = group * each + place * 2 * height
            blocks.append(sums[start:start + height] + sums[start + height:start + 2 * height])
        results.append(jnp.concatenate(blocks, axis=1)[0:9])
    return results


def send_wanted(out_ref, precond, ids, scalar):
    cameras = precond.shape[1]
    for pair in range(out_ref.shape[0] // 10):
        own = ids[:, pair * LANES:(pair + 1) * LANES]
        low = jnp.broadcast_to(own & (LANES - 1), (8, LANES))
        high = jnp.broadcast_to(own >> 7, (8, LANES))
        head = jnp.zeros((8, LANES), F32)
        tail = jnp.zeros((8, LANES), F32)
        for block in range(cameras // LANES):
            lanes = slice(block * LANES, (block + 1) * LANES)
            hit = high == block
            head = jnp.where(hit, take_lanes(precond[0:8, lanes], low), head)
            last = jnp.broadcast_to(precond[8:9, lanes], (8, LANES))
            tail = jnp.where(hit, take_lanes(last, low), tail)
        store_five(out_ref, pair, head, tail[0:1], scalar)


def owner_start_kernel(in_ref, damp_ref, out_ref, residual_ref, scaling_ref, precond_ref, ids_ref):
    rhs, diag, ids = [], [], []
    left = left_half(9)
    for pair in range(in_ref.shape[0] // 20):
        even = in_ref[20 * pair:20 * pair + 9]
        odd = in_ref[20 * pair + 10:20 * pair + 19]
        low = jnp.where(left, even, swap_halves(odd))
        high = jnp.where(left, swap_halves(even), odd)
        pad = jnp.zeros((7, LANES), F32)
        rhs.append(jnp.concatenate([low, pad], axis=0))
        diag.append(jnp.concatenate([high, pad], axis=0))
        even = in_ref[20 * pair + 9:20 * pair + 10]
        odd = in_ref[20 * pair + 19:20 * pair + 20]
        ids.append(jnp.where(left_half(1), even, swap_halves(odd)).astype(jnp.int32))
    ids = jnp.concatenate(ids, axis=1)
    ids_ref[...] = ids
    rhs = jnp.concatenate(rhs, axis=1)
    diag = jnp.concatenate(diag, axis=1)
    residual, diag = owner_sums([rhs, diag], ids, damp_ref.shape[1])
    scaling = diag + damp_ref[...]
    precond = residual / scaling
    residual_ref[...] = residual
    scaling_ref[...] = scaling
    precond_ref[...] = precond
    send_wanted(out_ref, precond, ids, sum_all(residual * precond))


def owner_image(in_ref, ids, cameras):
    image = []
    pad = jnp.zeros((7, LANES), F32)
    for pair in range(in_ref.shape[0] // 10):
        head, tail = load_five(in_ref, pair)
        image.append(jnp.concatenate([head, tail, pad], axis=0))
    return owner_sums([jnp.concatenate(image, axis=1)], ids, cameras)[0]


def owner_middle_kernel(in_ref, ids_ref, rz_ref, damp_ref, direction_ref, residual_ref, scaling_ref,
                        out_ref, update_ref, newres_ref, precond_ref):
    ids = ids_ref[...]
    direction = direction_ref[...]
    image = owner_image(in_ref, ids, damp_ref.shape[1]) + damp_ref[...] * direction
    step = rz_ref[0:1, 0:1] / carried_scalar(in_ref)
    update_ref[...] = step * direction
    residual = residual_ref[...] - step * image
    precond = residual / scaling_ref[...]
    newres_ref[...] = residual
    precond_ref[...] = precond
    send_wanted(out_ref, precond, ids, sum_all(residual * precond))


def owner_end_kernel(in_ref, ids_ref, rz_ref, damp_ref, direction_ref, residual_ref, update_ref,
                     newupdate_ref, newres_ref):
    direction = direction_ref[...]
    image = owner_image(in_ref, ids_ref[...], damp_ref.shape[1]) + damp_ref[...] * direction
    step = rz_ref[0:1, 0:1] / carried_scalar(in_ref)
    newupdate_ref[...] = update_ref[...] + step * direction
    newres_ref[...] = residual_ref[...] - step * image


def call(kernel, outs, scratch, *args, smem=0, hbm=0):
    whole = pl.BlockSpec(memory_space=pltpu.VMEM)
    specs = [pl.BlockSpec(memory_space=pltpu.SMEM)] * smem + [pl.BlockSpec(memory_space=pltpu.HBM)] * hbm
    specs += [whole] * (len(args) - smem - hbm)
    return pl.pallas_call(
        kernel,
        out_shape=[jax.ShapeDtypeStruct(shape, dtype) for shape, dtype in outs],
        in_specs=specs,
        out_specs=[whole] * len(outs),
        scratch_shapes=scratch,
        compiler_params=pltpu.CompilerParams(vmem_limit_bytes=VMEM_BYTES),
    )(*args)


def exchange(blocks, shards):
    moved = lax.all_to_all(blocks.reshape(shards, 1, -1), AXES, split_axis=0, concat_axis=0, tiled=True)
    return moved.reshape(blocks.shape)


def product_scratch(point_rows, slot_rows, nobs):
    return [pltpu.VMEM((rows, nobs), BF16) for rows in (point_rows, slot_rows)]


def start_call(chunk, *args):
    jac_cam, request, cam_damp = args[1], args[6], args[8]
    nobs = jac_cam.shape[1]
    shards = request.shape[0]
    groups = shards * CAP // 256
    copied = args[1:]
    rows = groups * 32 + (groups + 7) // 8 * 32
    scratch = [pltpu.VMEM((224, LANES), F32), pltpu.VMEM((rows, 256), F32), pltpu.VMEM((3, 8, LANES), F32)]
    scratch += product_scratch(224, rows, nobs)
    scratch += [pltpu.VMEM(arg.shape, arg.dtype) for arg in copied[:-1]]
    scratch += [pltpu.SemaphoreType.DMA] * len(copied)
    outs = [((shards * 10, LANES), F32), ((24, nobs), F32), ((8, nobs), F32), ((8, nobs), jnp.int32),
            ((nobs, LANES), BF16), ((nobs, 256), BF16), ((6, 8, LANES), F32), (cam_damp.shape, F32)]
    copied = [pltpu.with_memory_space_constraint(arg, pltpu.HBM) for arg in copied]
    return call(functools.partial(start_kernel, chunk), outs, scratch, args[0], *copied, smem=1, hbm=len(copied))


def apply_call(chunk, first, *args):
    arrived, camp = args[:2]
    nobs = camp.shape[1]
    shards = arrived.shape[0] // 5
    pairs = shards // 2
    groups = shards // 4
    cameras = args[7].shape[1]
    rows = groups * 16 + (groups + 7) // 8 * 16
    scratch = [pltpu.VMEM((80, LANES), F32), pltpu.VMEM((rows, 256), F32), pltpu.VMEM((3, 8, LANES), F32),
               pltpu.VMEM((8, nobs), F32)]
    scratch += product_scratch(80, rows, nobs)
    table = (pairs, 8, LANES)
    last = ((pairs + 7) // 8 * 8, LANES)
    scalar = ((8, LANES), F32)
    sent = ((shards * 5, LANES), F32)
    if first:
        outs = [sent, (table, F32), (last, F32), scalar]
    else:
        outs = [sent, ((9, cameras), F32), scalar]
        scratch += [pltpu.VMEM(table, F32), pltpu.VMEM(last, F32)]
    return call(functools.partial(apply_kernel, chunk, first), outs, scratch, *args)


def body(jac_cam, jac_pt, obs_residual, obs_point, obs_slot, request, obs_count, cam_damp, pt_damp):
    nobs = jac_cam.shape[1]
    shards = request.shape[0]
    cameras = cam_damp.shape[1]
    slots = shards * CAP
    chunk = 1024
    own = ((9, cameras), F32)
    sent = ((shards * 5, LANES), F32)
    sums, camp, jac, index, pointhot, slothot, inverse, damp = start_call(
        chunk, obs_count, jac_cam, jac_pt, obs_residual, obs_point.reshape(1, nobs), obs_slot.reshape(1, nobs),
        request, pt_damp.reshape(8, LANES), cam_damp)
    arrived = exchange(sums, shards)
    send, residual, scaling, precond, ids = call(
        owner_start_kernel, [sent, own, own, own, ((1, slots), jnp.int32)], [], arrived, damp)
    arrived = exchange(send, shards)
    send, table, last, rz = apply_call(
        chunk, True, arrived, camp, jac, index, pointhot, slothot, inverse, damp, precond)
    arrived = exchange(send, shards)
    direction = precond
    send, update, residual, precond = call(
        owner_middle_kernel, [sent, own, own, own], [],
        arrived, ids, rz, damp, direction, residual, scaling)
    arrived = exchange(send, shards)
    send, direction, rz = apply_call(
        chunk, False, arrived, camp, jac, index, pointhot, slothot, inverse, damp, precond, table, last, rz, direction)
    arrived = exchange(send, shards)
    update, residual = call(
        owner_end_kernel, [own, own], [], arrived, ids, rz, damp, direction, residual, update)
    return update, residual


def solution(mesh):
    wide = P(None, AXES)
    flat = P(AXES)
    return jax.shard_map(
        body,
        mesh=mesh,
        in_specs=(wide, wide, wide, flat, flat, P(AXES, None), flat, wide, flat),
        out_specs=(wide, wide),
        check_vma=False,
    )
```

```python
import functools

import jax
import jax.numpy as jnp
from jax import lax
from jax.experimental import pallas as pl
from jax.experimental.pallas import tpu as pltpu
from jax.sharding import PartitionSpec as P

AXES = ("cell", "img")
F32 = jnp.float32
BF16 = jnp.bfloat16
LANES = 128
CAP = 64
VMEM_BYTES = 32 * 1024 * 1024


def iota(shape, dim):
    return lax.broadcasted_iota(jnp.int32, shape, dim)


def take_lanes(table, lanes):
    return jnp.take_along_axis(table, lanes, axis=1, mode="promise_in_bounds")


def contract(left, right):
    return lax.dot_general(left, right, (((1,), (1,)), ((), ())), preferred_element_type=F32)


def one_hot_rows(index, rows):
    hit = iota((rows, index.shape[1]), 0) == index
    return jnp.where(hit, 1.0, 0.0).astype(BF16)


def one_hot_columns(index, columns):
    spread = jnp.broadcast_to(index.astype(F32), (LANES, LANES)).astype(BF16).T
    spread = jnp.concatenate([spread] * (columns // LANES), axis=1)
    lane = iota((LANES, columns), 1).astype(F32).astype(BF16)
    return jnp.where(spread == lane, jnp.ones((), BF16), jnp.zeros((), BF16))


def rounded_parts(value, count):
    parts = []
    for _ in range(count):
        part = value.astype(BF16)
        parts.append(part)
        value = value - part.astype(F32)
    return parts


def masked_rows(rows, hit):
    return [jnp.where(hit, jnp.broadcast_to(row, hit.shape), 0.0) for row in rows]


def stack_tiles(blocks):
    if len(blocks) % 2:
        blocks = blocks + [jnp.zeros_like(blocks[0])]
    return jnp.concatenate(blocks, axis=0).astype(BF16)


def group_hits(group):
    return jnp.broadcast_to(group, (8, group.shape[1])) == iota((8, group.shape[1]), 0)


def spread_slots(heads, tails, group, groups):
    width = group.shape[1]
    tiles = [jnp.concatenate(parts, axis=0).astype(BF16) for parts in heads]
    rows = []
    wide = jnp.broadcast_to(group, (8, width))
    for number in range(groups):
        hit = jnp.where(wide == number, 1.0, 0.0)
        hit = jnp.concatenate([hit, hit], axis=0).astype(BF16)
        rows += [tile * hit for tile in tiles]
    last = []
    for base in range(0, groups, 8):
        hit = wide == iota((8, width), 0) + base
        last += masked_rows(tails, hit)
    return jnp.concatenate(rows + [stack_tiles(last)], axis=0)


def wide_parts(value, count):
    return [part.astype(F32) for part in rounded_parts(value, count)]


def swap_halves(value):
    return pltpu.roll(value, CAP, 1)


def left_half(rows=8):
    return iota((rows, LANES), 1) < CAP


def sum_all(value):
    return jnp.sum(jnp.sum(value, axis=1, keepdims=True), axis=0, keepdims=True)


def carried_scalar(ref):
    total = ref[4:5, :]
    for sender in range(1, ref.shape[0] // 5):
        total = total + ref[5 * sender + 4:5 * sender + 5, :]
    return total[:, CAP:CAP + 1]


def store_five(out_ref, pair, head, tail, scalar):
    left = left_half()
    turned = swap_halves(head)
    even = jnp.where(left, head, pltpu.roll(turned, 4, 0))
    odd = jnp.where(left, turned, pltpu.roll(head, 4, 0))
    last = jnp.broadcast_to(tail, (8, LANES))
    last_even = jnp.where(left, last, scalar)
    last_odd = jnp.where(left, swap_halves(last), scalar)
    out_ref[10 * pair:10 * pair + 4] = even[0:4]
    out_ref[10 * pair + 4:10 * pair + 5] = last_even[0:1]
    out_ref[10 * pair + 5:10 * pair + 9] = odd[0:4]
    out_ref[10 * pair + 9:10 * pair + 10] = last_odd[0:1]


def load_five(in_ref, pair):
    left = left_half(4)
    even = in_ref[10 * pair:10 * pair + 4]
    odd = in_ref[10 * pair + 5:10 * pair + 9]
    low = jnp.where(left, even, swap_halves(odd))
    high = jnp.where(left, swap_halves(even), odd)
    last_even = in_ref[10 * pair + 4:10 * pair + 5]
    last_odd = in_ref[10 * pair + 9:10 * pair + 10]
    tail = jnp.where(left_half(1), last_even, swap_halves(last_odd))
    return jnp.concatenate([low, high], axis=0), tail


def pipelined(steps, build, product):
    for step in range(steps):
        build(step)
        if step:
            product(step - 1)
    product(steps - 1)


def chunk_lanes(step, chunk):
    return slice(step * chunk, (step + 1) * chunk)


def add_product(sums_ref, left_ref, right_ref, lanes, first):
    product = jnp.dot(left_ref[:, lanes], right_ref[lanes, :], preferred_element_type=F32)
    if first:
        sums_ref[...] = product
    else:
        sums_ref[...] += product


def point_spread(solved_ref, low, group, jac):
    low = jnp.broadcast_to(low, (8, LANES))
    hit = group_hits(group)
    first = jnp.zeros((8, LANES), F32)
    second = jnp.zeros((8, LANES), F32)
    for axis in range(3):
        taken = jnp.where(hit, take_lanes(solved_ref[axis], low), 0.0)
        first = first + jac[axis:axis + 1] * taken
        second = second + jac[axis + 4:axis + 5] * taken
    return jnp.sum(first, axis=0, keepdims=True), jnp.sum(second, axis=0, keepdims=True)


def two_level(jac, first, second):
    both = jac * jnp.where(iota(jac.shape, 0) < 4, first, second)
    return both + pltpu.roll(both, 4, 0)


def kept_rows(solved_ref, index_ref, jac_ref, along_ref, start, chunk):
    kept_a, kept_b = [], []
    for tile in range(chunk // LANES):
        spot = slice(start + tile * LANES, start + (tile + 1) * LANES)
        first, second = point_spread(solved_ref, index_ref[0:1, spot], index_ref[1:2, spot], jac_ref[:, spot])
        kept_a.append(along_ref[0:1, spot] - first)
        kept_b.append(along_ref[1:2, spot] - second)
    return jnp.concatenate(kept_a, axis=1), jnp.concatenate(kept_b, axis=1)


def solve_points(inverse_ref, totals, solved_ref):
    rows = ((0, 3, 5), (3, 1, 4), (5, 4, 2))
    for axis in range(3):
        solved_ref[axis] = (
            inverse_ref[rows[axis][0]] * totals[0]
            + inverse_ref[rows[axis][1]] * totals[1]
            + inverse_ref[rows[axis][2]] * totals[2]
        )


def summed_parts(sums_ref, start, rows, count, step):
    total = sums_ref[start:start + rows, :]
    for part in range(1, count):
        begin = start + part * step
        total = total + sums_ref[begin:begin + rows, :]
    return total


def start_kernel(chunk, count_ref, cam_hbm, pt_hbm, err_hbm, point_hbm, slot_hbm, req_hbm, damp_hbm, camdamp_hbm,
                 out_ref, camp_ref, jac_ref, index_ref, pointhot_ref, slothot_ref, inverse_ref, camdamp_ref,
                 psum_ref, ssum_ref, solved_ref, pointrows_ref, slotrows_ref,
                 cam_ref, pt_ref, err_ref, point_ref, slot_ref, req_ref, damp_ref,
                 cam_sem, pt_sem, err_sem, point_sem, slot_sem, req_sem, damp_sem, camdamp_sem):
    nobs = cam_ref.shape[1]
    steps = nobs // chunk
    copies = [
        pltpu.make_async_copy(point_hbm, point_ref, point_sem),
        pltpu.make_async_copy(slot_hbm, slot_ref, slot_sem),
        pltpu.make_async_copy(pt_hbm, pt_ref, pt_sem),
        pltpu.make_async_copy(err_hbm, err_ref, err_sem),
        pltpu.make_async_copy(damp_hbm, damp_ref, damp_sem),
        pltpu.make_async_copy(cam_hbm, cam_ref, cam_sem),
        pltpu.make_async_copy(req_hbm, req_ref, req_sem),
        pltpu.make_async_copy(camdamp_hbm, camdamp_ref, camdamp_sem),
    ]
    for copy in copies:
        copy.start()
    count = count_ref[0]
    groups = req_ref.shape[0] * CAP // 256
    for copy in copies[:2]:
        copy.wait()

    for step in range(steps):
        lanes = chunk_lanes(step, chunk)
        live = iota((1, chunk), 1) + step * chunk < count
        point = point_ref[:, lanes]
        low = point & (LANES - 1)
        group = jnp.where(live, point >> 7, -1)
        slot = slot_ref[:, lanes]
        index_ref[0:1, lanes] = low
        index_ref[1:2, lanes] = group
        index_ref[2:3, lanes] = slot
        index_ref[3:4, lanes] = jnp.where(live, slot >> 8, -1)
        for tile in range(chunk // LANES):
            spot = slice(step * chunk + tile * LANES, step * chunk + (tile + 1) * LANES)
            part = chunk_lanes(tile, LANES)
            pointhot_ref[spot, :] = one_hot_columns(low[:, part], LANES)
            slothot_ref[spot, :] = one_hot_columns(slot[:, part] & 255, 256)
    for copy in copies[2:5]:
        copy.wait()

    def build_points(step):
        lanes = chunk_lanes(step, chunk)
        group = index_ref[1:2, lanes]
        jac = pt_ref[:, lanes]
        zero = jnp.zeros((1, chunk), F32)
        jac_ref[:, lanes] = jnp.concatenate([jac[0:3], zero, jac[3:6], zero], axis=0)
        jac_a = jnp.concatenate([jac[0:3], zero, jac[0:3], zero], axis=0)
        jac_b = jnp.concatenate([jac[3:6], zero, jac[3:6], zero], axis=0)
        turn_a = jnp.concatenate([jac[0:3], zero, jac[1:3], jac[0:1], zero], axis=0)
        turn_b = jnp.concatenate([jac[3:6], zero, jac[4:6], jac[3:4], zero], axis=0)
        err = err_ref[:, lanes]
        blocks = wide_parts(jac_a * turn_a + jac_b * turn_b, 3)
        sides = wide_parts(jac_a * err[0:1] + jac_b * err[1:2], 3)
        rows = [block[place:place + 1] for block in blocks for place in (0, 1, 2, 4, 5, 6)]
        rows += [side[place:place + 1] for side in sides for place in (0, 1, 2)]
        pointrows_ref[:, lanes] = stack_tiles(masked_rows(rows, group_hits(group)))

    pipelined(steps, build_points, lambda step: add_product(
        psum_ref, pointrows_ref, pointhot_ref, chunk_lanes(step, chunk), step == 0))

    damp = damp_ref[...]
    m00, m11, m22, m01, m12, m20 = [summed_parts(psum_ref, 8 * place, 8, 3, 48) for place in range(6)]
    m00, m11, m22 = m00 + damp, m11 + damp, m22 + damp
    c00 = m11 * m22 - m12 * m12
    c01 = m12 * m20 - m01 * m22
    c02 = m01 * m12 - m11 * m20
    c11 = m22 * m00 - m20 * m20
    c12 = m20 * m01 - m12 * m00
    c22 = m00 * m11 - m01 * m01
    det = m00 * c00 + m01 * c01 + m20 * c02
    for place, cofactor in enumerate((c00, c11, c22, c01, c12, c02)):
        inverse_ref[place] = cofactor / det
    solve_points(inverse_ref, [summed_parts(psum_ref, 144 + 8 * place, 8, 3, 24) for place in range(3)], solved_ref)
    for copy in copies[5:]:
        copy.wait()

    def build_slots(step):
        lanes = chunk_lanes(step, chunk)
        cam_a = cam_ref[0:8, lanes]
        cam_b = cam_ref[9:17, lanes]
        last = jnp.concatenate([cam_ref[8:9, lanes], cam_ref[17:18, lanes], jnp.zeros((6, chunk), F32)], axis=0)
        camp_ref[0:8, lanes] = cam_a
        camp_ref[8:16, lanes] = cam_b
        camp_ref[16:24, lanes] = last
        kept_a, kept_b = kept_rows(solved_ref, index_ref, jac_ref, err_ref, step * chunk, chunk)
        rhs = wide_parts(-(cam_a * kept_a + cam_b * kept_b), 2)
        diag = wide_parts(cam_a * cam_a + cam_b * cam_b, 2)
        last_a, last_b = last[0:1], last[1:2]
        tails = wide_parts(-(last_a * kept_a + last_b * kept_b), 2) + wide_parts(last_a * last_a + last_b * last_b, 2)
        slotrows_ref[:, lanes] = spread_slots([rhs, diag], tails, index_ref[3:4, lanes], groups)

    pipelined(steps, build_slots, lambda step: add_product(
        ssum_ref, slotrows_ref, slothot_ref, chunk_lanes(step, chunk), step == 0))
    wanted = req_ref[...].astype(F32)
    wanted = jnp.concatenate([wanted, jnp.zeros_like(wanted)], axis=1)
    left = left_half()
    left_one = left_half(1)
    for group in range(groups):
        rhs = summed_parts(ssum_ref, 32 * group, 8, 2, 8)
        diag = summed_parts(ssum_ref, 32 * group + 16, 8, 2, 8)
        last = 32 * groups + 32 * (group // 8) + group % 8
        rhs_last = summed_parts(ssum_ref, last, 1, 2, 8)
        diag_last = summed_parts(ssum_ref, last + 16, 1, 2, 8)
        for half in range(2):
            lanes = slice(half * LANES, (half + 1) * LANES)
            row = 20 * (2 * group + half)
            out_ref[row:row + 8] = jnp.where(left, rhs[:, lanes], swap_halves(diag[:, lanes]))
            out_ref[row + 10:row + 18] = jnp.where(left, swap_halves(rhs[:, lanes]), diag[:, lanes])
            out_ref[row + 8:row + 9] = jnp.where(left_one, rhs_last[:, lanes], swap_halves(diag_last[:, lanes]))
            out_ref[row + 18:row + 19] = jnp.where(left_one, swap_halves(rhs_last[:, lanes]), diag_last[:, lanes])
            owner = 4 * group + 2 * half
            out_ref[row + 9:row + 10] = wanted[owner:owner + 1]
            out_ref[row + 19:row + 20] = wanted[owner + 1:owner + 2]


def apply_kernel(chunk, first, *refs):
    if first:
        (in_ref, camp_ref, jac_ref, index_ref, pointhot_ref, slothot_ref, inverse_ref, damp_ref, precond_ref,
         out_ref, table_ref, last_ref, rz_ref, *work) = refs
    else:
        (in_ref, camp_ref, jac_ref, index_ref, pointhot_ref, slothot_ref, inverse_ref, damp_ref, precond_ref,
         oldtable_ref, oldlast_ref, oldrz_ref, oldown_ref,
         out_ref, own_ref, rz_ref, *work, table_ref, last_ref) = refs
    psum_ref, ssum_ref, solved_ref, along_ref, pointrows_ref, slotrows_ref = work
    nobs = camp_ref.shape[1]
    steps = nobs // chunk
    pairs = table_ref.shape[0]
    groups = pairs // 2
    rz = carried_scalar(in_ref)
    rz_ref[...] = jnp.broadcast_to(rz, rz_ref.shape)
    own = precond_ref[...]
    if not first:
        beta = rz / oldrz_ref[0:1, 0:1]
        own = own + beta * oldown_ref[...]
        own_ref[...] = own
    for pair in range(pairs):
        head, tail = load_five(in_ref, pair)
        if not first:
            head = head + beta * oldtable_ref[pair]
            tail = tail + beta * oldlast_ref[pair:pair + 1]
        table_ref[pair] = head
        last_ref[pair:pair + 1] = tail

    def build_points(step):
        lanes = chunk_lanes(step, chunk)
        for tile in range(chunk // LANES):
            spot = slice(step * chunk + tile * LANES, step * chunk + (tile + 1) * LANES)
            slot = index_ref[2:3, spot]
            low = jnp.broadcast_to(slot & (LANES - 1), (8, LANES))
            high = jnp.broadcast_to(slot >> 7, (8, LANES))
            taken = jnp.zeros((8, LANES), F32)
            for pair in range(pairs):
                taken = jnp.where(high == pair, take_lanes(table_ref[pair], low), taken)
            tail = jnp.zeros((8, LANES), F32)
            for base in range(0, pairs, 8):
                hit = high == iota((8, LANES), 0) + base
                tail = jnp.where(hit, take_lanes(last_ref[base:base + 8], low), tail)
            tail = jnp.sum(tail, axis=0, keepdims=True)
            along_ref[0:1, spot] = jnp.sum(camp_ref[0:8, spot] * taken, axis=0, keepdims=True) + camp_ref[16:17, spot] * tail
            along_ref[1:2, spot] = jnp.sum(camp_ref[8:16, spot] * taken, axis=0, keepdims=True) + camp_ref[17:18, spot] * tail
        sides = wide_parts(two_level(jac_ref[:, lanes], along_ref[0:1, lanes], along_ref[1:2, lanes]), 3)
        rows = [side[place:place + 1] for side in sides for place in (0, 1, 2)]
        pointrows_ref[:, lanes] = stack_tiles(masked_rows(rows, group_hits(index_ref[1:2, lanes])))

    pipelined(steps, build_points, lambda step: add_product(
        psum_ref, pointrows_ref, pointhot_ref, chunk_lanes(step, chunk), step == 0))
    solve_points(inverse_ref, [summed_parts(psum_ref, 8 * place, 8, 3, 24) for place in range(3)], solved_ref)
    energies = []

    def build_slots(step):
        lanes = chunk_lanes(step, chunk)
        kept_a, kept_b = kept_rows(solved_ref, index_ref, jac_ref, along_ref, step * chunk, chunk)
        heads = wide_parts(camp_ref[0:8, lanes] * kept_a + camp_ref[8:16, lanes] * kept_b, 2)
        tails = wide_parts(camp_ref[16:17, lanes] * kept_a + camp_ref[17:18, lanes] * kept_b, 2)
        group = index_ref[3:4, lanes]
        slotrows_ref[:, lanes] = spread_slots([heads], tails, group, groups)
        energy = along_ref[0:1, lanes] * kept_a + along_ref[1:2, lanes] * kept_b
        energies.append(jnp.where(group >= 0, energy, 0.0))

    pipelined(steps, build_slots, lambda step: add_product(
        ssum_ref, slotrows_ref, slothot_ref, chunk_lanes(step, chunk), step == 0))
    energy = energies[0]
    for more in energies[1:]:
        energy = energy + more
    partial = sum_all(energy) + sum_all(damp_ref[...] * own * own)
    for group in range(groups):
        head = summed_parts(ssum_ref, 16 * group, 8, 2, 8)
        tail = summed_parts(ssum_ref, 16 * groups + 16 * (group // 8) + group % 8, 1, 2, 8)
        for half in range(2):
            lanes = slice(half * LANES, (half + 1) * LANES)
            store_five(out_ref, 2 * group + half, head[:, lanes], tail[:, lanes], partial)


def owner_sums(values, ids, cameras):
    groups = cameras // 256
    tiles = []
    for value in values:
        parts = wide_parts(value, 2)
        tiles.append(jnp.concatenate(parts, axis=0).astype(BF16))
    rows = []
    for number in range(groups):
        hit = jnp.where(jnp.broadcast_to(ids >> 8, tiles[0].shape) == number, 1.0, 0.0).astype(BF16)
        rows += [tile * hit for tile in tiles]
    sums = contract(jnp.concatenate(rows, axis=0), one_hot_rows(ids & 255, 256))
    results = []
    height = values[0].shape[0]
    each = 2 * height * len(tiles)
    for place in range(len(values)):
        blocks = []
        for group in range(groups):
            start = group * each + place * 2 * height
            blocks.append(sums[start:start + height] + sums[start + height:start + 2 * height])
        results.append(jnp.concatenate(blocks, axis=1)[0:9])
    return results


def send_wanted(out_ref, precond, ids, scalar):
    cameras = precond.shape[1]
    blocks = cameras // LANES
    spare = [jnp.zeros((1, LANES), F32)] * (8 - blocks)
    last = jnp.concatenate([precond[8:9, block * LANES:(block + 1) * LANES] for block in range(blocks)] + spare, axis=0)
    for pair in range(out_ref.shape[0] // 10):
        own = ids[:, pair * LANES:(pair + 1) * LANES]
        low = jnp.broadcast_to(own & (LANES - 1), (8, LANES))
        high = jnp.broadcast_to(own >> 7, (8, LANES))
        head = jnp.zeros((8, LANES), F32)
        for block in range(blocks):
            head = jnp.where(high == block, take_lanes(precond[0:8, block * LANES:(block + 1) * LANES], low), head)
        tail = jnp.where(high == iota((8, LANES), 0), take_lanes(last, low), 0.0)
        store_five(out_ref, pair, head, jnp.sum(tail, axis=0, keepdims=True), scalar)


def owner_start_kernel(in_ref, damp_ref, out_ref, residual_ref, scaling_ref, precond_ref, ids_ref):
    rhs, diag, ids = [], [], []
    left = left_half(9)
    for pair in range(in_ref.shape[0] // 20):
        even = in_ref[20 * pair:20 * pair + 9]
        odd = in_ref[20 * pair + 10:20 * pair + 19]
        low = jnp.where(left, even, swap_halves(odd))
        high = jnp.where(left, swap_halves(even), odd)
        pad = jnp.zeros((7, LANES), F32)
        rhs.append(jnp.concatenate([low, pad], axis=0))
        diag.append(jnp.concatenate([high, pad], axis=0))
        even = in_ref[20 * pair + 9:20 * pair + 10]
        odd = in_ref[20 * pair + 19:20 * pair + 20]
        ids.append(jnp.where(left_half(1), even, swap_halves(odd)).astype(jnp.int32))
    ids = jnp.concatenate(ids, axis=1)
    ids_ref[...] = ids
    rhs = jnp.concatenate(rhs, axis=1)
    diag = jnp.concatenate(diag, axis=1)
    residual, diag = owner_sums([rhs, diag], ids, damp_ref.shape[1])
    scaling = diag + damp_ref[...]
    precond = residual / scaling
    residual_ref[...] = residual
    scaling_ref[...] = scaling
    precond_ref[...] = precond
    send_wanted(out_ref, precond, ids, sum_all(residual * precond))


def owner_image(in_ref, ids, cameras):
    image = []
    pad = jnp.zeros((7, LANES), F32)
    for pair in range(in_ref.shape[0] // 10):
        head, tail = load_five(in_ref, pair)
        image.append(jnp.concatenate([head, tail, pad], axis=0))
    return owner_sums([jnp.concatenate(image, axis=1)], ids, cameras)[0]


def owner_middle_kernel(in_ref, ids_ref, rz_ref, damp_ref, direction_ref, residual_ref, scaling_ref,
                        out_ref, update_ref, newres_ref, precond_ref):
    ids = ids_ref[...]
    direction = direction_ref[...]
    image = owner_image(in_ref, ids, damp_ref.shape[1]) + damp_ref[...] * direction
    step = rz_ref[0:1, 0:1] / carried_scalar(in_ref)
    update_ref[...] = step * direction
    residual = residual_ref[...] - step * image
    precond = residual / scaling_ref[...]
    newres_ref[...] = residual
    precond_ref[...] = precond
    send_wanted(out_ref, precond, ids, sum_all(residual * precond))


def owner_end_kernel(in_ref, ids_ref, rz_ref, damp_ref, direction_ref, residual_ref, update_ref,
                     newupdate_ref, newres_ref):
    direction = direction_ref[...]
    image = owner_image(in_ref, ids_ref[...], damp_ref.shape[1]) + damp_ref[...] * direction
    step = rz_ref[0:1, 0:1] / carried_scalar(in_ref)
    newupdate_ref[...] = update_ref[...] + step * direction
    newres_ref[...] = residual_ref[...] - step * image


def call(kernel, outs, scratch, *args, smem=0, hbm=0):
    whole = pl.BlockSpec(memory_space=pltpu.VMEM)
    specs = [pl.BlockSpec(memory_space=pltpu.SMEM)] * smem + [pl.BlockSpec(memory_space=pltpu.HBM)] * hbm
    specs += [whole] * (len(args) - smem - hbm)
    return pl.pallas_call(
        kernel,
        out_shape=[jax.ShapeDtypeStruct(shape, dtype) for shape, dtype in outs],
        in_specs=specs,
        out_specs=[whole] * len(outs),
        scratch_shapes=scratch,
        compiler_params=pltpu.CompilerParams(vmem_limit_bytes=VMEM_BYTES),
    )(*args)


def exchange(blocks, shards):
    moved = lax.all_to_all(blocks.reshape(shards, 1, -1), AXES, split_axis=0, concat_axis=0, tiled=True)
    return moved.reshape(blocks.shape)


def product_scratch(point_rows, slot_rows, nobs):
    return [pltpu.VMEM((rows, nobs), BF16) for rows in (point_rows, slot_rows)]


def start_call(chunk, *args):
    jac_cam, request, cam_damp = args[1], args[6], args[8]
    nobs = jac_cam.shape[1]
    shards = request.shape[0]
    groups = shards * CAP // 256
    copied = args[1:]
    rows = groups * 32 + (groups + 7) // 8 * 32
    scratch = [pltpu.VMEM((224, LANES), F32), pltpu.VMEM((rows, 256), F32), pltpu.VMEM((3, 8, LANES), F32)]
    scratch += product_scratch(224, rows, nobs)
    scratch += [pltpu.VMEM(arg.shape, arg.dtype) for arg in copied[:-1]]
    scratch += [pltpu.SemaphoreType.DMA] * len(copied)
    outs = [((shards * 10, LANES), F32), ((24, nobs), F32), ((8, nobs), F32), ((8, nobs), jnp.int32),
            ((nobs, LANES), BF16), ((nobs, 256), BF16), ((6, 8, LANES), F32), (cam_damp.shape, F32)]
    copied = [pltpu.with_memory_space_constraint(arg, pltpu.HBM) for arg in copied]
    return call(functools.partial(start_kernel, chunk), outs, scratch, args[0], *copied, smem=1, hbm=len(copied))


def apply_call(chunk, first, *args):
    arrived, camp = args[:2]
    nobs = camp.shape[1]
    shards = arrived.shape[0] // 5
    pairs = shards // 2
    groups = shards // 4
    cameras = args[7].shape[1]
    rows = groups * 16 + (groups + 7) // 8 * 16
    scratch = [pltpu.VMEM((80, LANES), F32), pltpu.VMEM((rows, 256), F32), pltpu.VMEM((3, 8, LANES), F32),
               pltpu.VMEM((8, nobs), F32)]
    scratch += product_scratch(80, rows, nobs)
    table = (pairs, 8, LANES)
    last = ((pairs + 7) // 8 * 8, LANES)
    scalar = ((8, LANES), F32)
    sent = ((shards * 5, LANES), F32)
    if first:
        outs = [sent, (table, F32), (last, F32), scalar]
    else:
        outs = [sent, ((9, cameras), F32), scalar]
        scratch += [pltpu.VMEM(table, F32), pltpu.VMEM(last, F32)]
    return call(functools.partial(apply_kernel, chunk, first), outs, scratch, *args)


def body(jac_cam, jac_pt, obs_residual, obs_point, obs_slot, request, obs_count, cam_damp, pt_damp):
    nobs = jac_cam.shape[1]
    shards = request.shape[0]
    cameras = cam_damp.shape[1]
    slots = shards * CAP
    start_chunk, chunk = 512, 256
    own = ((9, cameras), F32)
    sent = ((shards * 5, LANES), F32)
    sums, camp, jac, index, pointhot, slothot, inverse, damp = start_call(
        start_chunk, obs_count, jac_cam, jac_pt, obs_residual, obs_point.reshape(1, nobs), obs_slot.reshape(1, nobs),
        request, pt_damp.reshape(8, LANES), cam_damp)
    arrived = exchange(sums, shards)
    send, residual, scaling, precond, ids = call(
        owner_start_kernel, [sent, own, own, own, ((1, slots), jnp.int32)], [], arrived, damp)
    arrived = exchange(send, shards)
    send, table, last, rz = apply_call(
        chunk, True, arrived, camp, jac, index, pointhot, slothot, inverse, damp, precond)
    arrived = exchange(send, shards)
    direction = precond
    send, update, residual, precond = call(
        owner_middle_kernel, [sent, own, own, own], [],
        arrived, ids, rz, damp, direction, residual, scaling)
    arrived = exchange(send, shards)
    send, direction, rz = apply_call(
        chunk, False, arrived, camp, jac, index, pointhot, slothot, inverse, damp, precond, table, last, rz, direction)
    arrived = exchange(send, shards)
    update, residual = call(
        owner_end_kernel, [own, own], [], arrived, ids, rz, damp, direction, residual, update)
    return update, residual


def solution(mesh):
    wide = P(None, AXES)
    flat = P(AXES)
    return jax.shard_map(
        body,
        mesh=mesh,
        in_specs=(wide, wide, wide, flat, flat, P(AXES, None), flat, wide, flat),
        out_specs=(wide, wide),
        check_vma=False,
    )
```

```python
import functools

import jax
import jax.numpy as jnp
from jax import lax
from jax.experimental import pallas as pl
from jax.experimental.pallas import tpu as pltpu
from jax.sharding import PartitionSpec as P

AXES = ("cell", "img")
F32 = jnp.float32
BF16 = jnp.bfloat16
LANES = 128
CAP = 64
VMEM_BYTES = 32 * 1024 * 1024


def iota(shape, dim):
    return lax.broadcasted_iota(jnp.int32, shape, dim)


def take_lanes(table, lanes):
    return jnp.take_along_axis(table, lanes, axis=1, mode="promise_in_bounds")


def take_tables(tables, low, high):
    bits = (len(tables) - 1).bit_length()
    hits = [(high & (1 << bit)) != 0 for bit in range(bits)]

    def pick(base, bit):
        if bit < 0:
            return take_lanes(tables[base](), low)
        other = base + (1 << bit)
        if other >= len(tables):
            return pick(base, bit - 1)
        return jnp.where(hits[bit], pick(other, bit - 1), pick(base, bit - 1))

    return pick(0, bits - 1)


def contract(left, right):
    return lax.dot_general(left, right, (((1,), (1,)), ((), ())), preferred_element_type=F32)


def one_hot_rows(index, rows):
    hit = iota((rows, index.shape[1]), 0) == index
    return jnp.where(hit, 1.0, 0.0).astype(BF16)


def one_hot_columns(index, columns):
    spread = jnp.broadcast_to(index.astype(F32), (LANES, LANES)).astype(BF16).T
    spread = jnp.concatenate([spread] * (columns // LANES), axis=1)
    lane = iota((LANES, columns), 1).astype(F32).astype(BF16)
    return jnp.where(spread == lane, jnp.ones((), BF16), jnp.zeros((), BF16))


def rounded_parts(value, count):
    parts = []
    for _ in range(count):
        part = value.astype(BF16)
        parts.append(part)
        value = value - part.astype(F32)
    return parts


def masked_rows(rows, hit):
    return [jnp.where(hit, jnp.broadcast_to(row, hit.shape), 0.0) for row in rows]


def stack_tiles(blocks):
    if len(blocks) % 2:
        blocks = blocks + [jnp.zeros_like(blocks[0])]
    return jnp.concatenate(blocks, axis=0).astype(BF16)


def group_hits(group):
    return jnp.broadcast_to(group, (8, group.shape[1])) == iota((8, group.shape[1]), 0)


def spread_slots(heads, tails, group, groups):
    width = group.shape[1]
    tiles = [jnp.concatenate(parts, axis=0).astype(BF16) for parts in heads]
    rows = []
    wide = jnp.broadcast_to(group, (8, width))
    for number in range(groups):
        hit = jnp.where(wide == number, 1.0, 0.0)
        hit = jnp.concatenate([hit, hit], axis=0).astype(BF16)
        rows += [tile * hit for tile in tiles]
    last = []
    for base in range(0, groups, 8):
        hit = wide == iota((8, width), 0) + base
        last += masked_rows(tails, hit)
    return jnp.concatenate(rows + [stack_tiles(last)], axis=0)


def wide_parts(value, count):
    return [part.astype(F32) for part in rounded_parts(value, count)]


def swap_halves(value):
    return pltpu.roll(value, CAP, 1)


def left_half(rows=8):
    return iota((rows, LANES), 1) < CAP


def sum_all(value):
    return jnp.sum(jnp.sum(value, axis=1, keepdims=True), axis=0, keepdims=True)


def carried_scalar(ref):
    total = ref[4:5, :]
    for sender in range(1, ref.shape[0] // 5):
        total = total + ref[5 * sender + 4:5 * sender + 5, :]
    return total[:, CAP:CAP + 1]


def store_five(out_ref, pair, head, tail, scalar):
    left = left_half()
    turned = swap_halves(head)
    even = jnp.where(left, head, pltpu.roll(turned, 4, 0))
    odd = jnp.where(left, turned, pltpu.roll(head, 4, 0))
    last = jnp.broadcast_to(tail, (8, LANES))
    last_even = jnp.where(left, last, scalar)
    last_odd = jnp.where(left, swap_halves(last), scalar)
    out_ref[10 * pair:10 * pair + 4] = even[0:4]
    out_ref[10 * pair + 4:10 * pair + 5] = last_even[0:1]
    out_ref[10 * pair + 5:10 * pair + 9] = odd[0:4]
    out_ref[10 * pair + 9:10 * pair + 10] = last_odd[0:1]


def load_five(in_ref, pair):
    left = left_half(4)
    even = in_ref[10 * pair:10 * pair + 4]
    odd = in_ref[10 * pair + 5:10 * pair + 9]
    low = jnp.where(left, even, swap_halves(odd))
    high = jnp.where(left, swap_halves(even), odd)
    last_even = in_ref[10 * pair + 4:10 * pair + 5]
    last_odd = in_ref[10 * pair + 9:10 * pair + 10]
    tail = jnp.where(left_half(1), last_even, swap_halves(last_odd))
    return jnp.concatenate([low, high], axis=0), tail


def pipelined(steps, build, product):
    for step in range(steps):
        build(step)
        if step:
            product(step - 1)
    product(steps - 1)


def chunk_lanes(step, chunk):
    return slice(step * chunk, (step + 1) * chunk)


def add_product(sums_ref, left_ref, right_ref, lanes, first):
    product = jnp.dot(left_ref[:, lanes], right_ref[lanes, :], preferred_element_type=F32)
    if first:
        sums_ref[...] = product
    else:
        sums_ref[...] += product


def point_spread(solved_ref, low, group, jac):
    low = jnp.broadcast_to(low, (8, LANES))
    hit = group_hits(group)
    first = jnp.zeros((8, LANES), F32)
    second = jnp.zeros((8, LANES), F32)
    for axis in range(3):
        taken = jnp.where(hit, take_lanes(solved_ref[axis], low), 0.0)
        first = first + jac[axis:axis + 1] * taken
        second = second + jac[axis + 4:axis + 5] * taken
    return jnp.sum(first, axis=0, keepdims=True), jnp.sum(second, axis=0, keepdims=True)


def two_level(jac, first, second):
    both = jac * jnp.where(iota(jac.shape, 0) < 4, first, second)
    return both + pltpu.roll(both, 4, 0)


def kept_rows(solved_ref, index_ref, jac_ref, along_ref, start, chunk):
    kept_a, kept_b = [], []
    for tile in range(chunk // LANES):
        spot = slice(start + tile * LANES, start + (tile + 1) * LANES)
        first, second = point_spread(solved_ref, index_ref[0:1, spot], index_ref[1:2, spot], jac_ref[:, spot])
        kept_a.append(along_ref[0:1, spot] - first)
        kept_b.append(along_ref[1:2, spot] - second)
    return jnp.concatenate(kept_a, axis=1), jnp.concatenate(kept_b, axis=1)


def solve_points(inverse_ref, totals, solved_ref):
    rows = ((0, 3, 5), (3, 1, 4), (5, 4, 2))
    for axis in range(3):
        solved_ref[axis] = (
            inverse_ref[rows[axis][0]] * totals[0]
            + inverse_ref[rows[axis][1]] * totals[1]
            + inverse_ref[rows[axis][2]] * totals[2]
        )


def summed_parts(sums_ref, start, rows, count, step):
    total = sums_ref[start:start + rows, :]
    for part in range(1, count):
        begin = start + part * step
        total = total + sums_ref[begin:begin + rows, :]
    return total


def start_kernel(chunk, count_ref, cam_hbm, pt_hbm, err_hbm, point_hbm, slot_hbm, req_hbm, damp_hbm, camdamp_hbm,
                 out_ref, camp_ref, jac_ref, index_ref, pointhot_ref, slothot_ref, inverse_ref, camdamp_ref,
                 psum_ref, ssum_ref, solved_ref, pointrows_ref, slotrows_ref,
                 cam_ref, pt_ref, err_ref, point_ref, slot_ref, req_ref, damp_ref,
                 cam_sem, pt_sem, err_sem, point_sem, slot_sem, req_sem, damp_sem, camdamp_sem):
    nobs = cam_ref.shape[1]
    steps = nobs // chunk
    copies = [
        pltpu.make_async_copy(point_hbm, point_ref, point_sem),
        pltpu.make_async_copy(slot_hbm, slot_ref, slot_sem),
        pltpu.make_async_copy(pt_hbm, pt_ref, pt_sem),
        pltpu.make_async_copy(err_hbm, err_ref, err_sem),
        pltpu.make_async_copy(damp_hbm, damp_ref, damp_sem),
        pltpu.make_async_copy(cam_hbm, cam_ref, cam_sem),
        pltpu.make_async_copy(req_hbm, req_ref, req_sem),
        pltpu.make_async_copy(camdamp_hbm, camdamp_ref, camdamp_sem),
    ]
    for copy in copies:
        copy.start()
    count = count_ref[0]
    groups = req_ref.shape[0] * CAP // 256
    for copy in copies[:2]:
        copy.wait()

    for step in range(steps):
        lanes = chunk_lanes(step, chunk)
        live = iota((1, chunk), 1) + step * chunk < count
        point = point_ref[:, lanes]
        low = point & (LANES - 1)
        group = jnp.where(live, point >> 7, -1)
        slot = slot_ref[:, lanes]
        index_ref[0:1, lanes] = low
        index_ref[1:2, lanes] = group
        index_ref[2:3, lanes] = slot
        index_ref[3:4, lanes] = jnp.where(live, slot >> 8, -1)
        for tile in range(chunk // LANES):
            spot = slice(step * chunk + tile * LANES, step * chunk + (tile + 1) * LANES)
            part = chunk_lanes(tile, LANES)
            pointhot_ref[spot, :] = one_hot_columns(low[:, part], LANES)
            slothot_ref[spot, :] = one_hot_columns(slot[:, part] & 255, 256)
    for copy in copies[2:5]:
        copy.wait()

    def build_points(step):
        lanes = chunk_lanes(step, chunk)
        group = index_ref[1:2, lanes]
        jac = pt_ref[:, lanes]
        zero = jnp.zeros((1, chunk), F32)
        jac_ref[:, lanes] = jnp.concatenate([jac[0:3], zero, jac[3:6], zero], axis=0)
        jac_a = jnp.concatenate([jac[0:3], zero, jac[0:3], zero], axis=0)
        jac_b = jnp.concatenate([jac[3:6], zero, jac[3:6], zero], axis=0)
        turn_a = jnp.concatenate([jac[0:3], zero, jac[1:3], jac[0:1], zero], axis=0)
        turn_b = jnp.concatenate([jac[3:6], zero, jac[4:6], jac[3:4], zero], axis=0)
        err = err_ref[:, lanes]
        blocks = wide_parts(jac_a * turn_a + jac_b * turn_b, 3)
        sides = wide_parts(jac_a * err[0:1] + jac_b * err[1:2], 3)
        rows = [block[place:place + 1] for block in blocks for place in (0, 1, 2, 4, 5, 6)]
        rows += [side[place:place + 1] for side in sides for place in (0, 1, 2)]
        pointrows_ref[:, lanes] = stack_tiles(masked_rows(rows, group_hits(group)))

    pipelined(steps, build_points, lambda step: add_product(
        psum_ref, pointrows_ref, pointhot_ref, chunk_lanes(step, chunk), step == 0))

    damp = damp_ref[...]
    m00, m11, m22, m01, m12, m20 = [summed_parts(psum_ref, 8 * place, 8, 3, 48) for place in range(6)]
    m00, m11, m22 = m00 + damp, m11 + damp, m22 + damp
    c00 = m11 * m22 - m12 * m12
    c01 = m12 * m20 - m01 * m22
    c02 = m01 * m12 - m11 * m20
    c11 = m22 * m00 - m20 * m20
    c12 = m20 * m01 - m12 * m00
    c22 = m00 * m11 - m01 * m01
    det = m00 * c00 + m01 * c01 + m20 * c02
    for place, cofactor in enumerate((c00, c11, c22, c01, c12, c02)):
        inverse_ref[place] = cofactor / det
    solve_points(inverse_ref, [summed_parts(psum_ref, 144 + 8 * place, 8, 3, 24) for place in range(3)], solved_ref)
    for copy in copies[5:]:
        copy.wait()

    def build_slots(step):
        lanes = chunk_lanes(step, chunk)
        cam_a = cam_ref[0:8, lanes]
        cam_b = cam_ref[9:17, lanes]
        last = jnp.concatenate([cam_ref[8:9, lanes], cam_ref[17:18, lanes], jnp.zeros((6, chunk), F32)], axis=0)
        camp_ref[0:8, lanes] = cam_a
        camp_ref[8:16, lanes] = cam_b
        camp_ref[16:24, lanes] = last
        kept_a, kept_b = kept_rows(solved_ref, index_ref, jac_ref, err_ref, step * chunk, chunk)
        rhs = wide_parts(-(cam_a * kept_a + cam_b * kept_b), 2)
        diag = wide_parts(cam_a * cam_a + cam_b * cam_b, 2)
        last_a, last_b = last[0:1], last[1:2]
        tails = wide_parts(-(last_a * kept_a + last_b * kept_b), 2) + wide_parts(last_a * last_a + last_b * last_b, 2)
        slotrows_ref[:, lanes] = spread_slots([rhs, diag], tails, index_ref[3:4, lanes], groups)

    pipelined(steps, build_slots, lambda step: add_product(
        ssum_ref, slotrows_ref, slothot_ref, chunk_lanes(step, chunk), step == 0))
    wanted = req_ref[...].astype(F32)
    wanted = jnp.concatenate([wanted, jnp.zeros_like(wanted)], axis=1)
    left = left_half()
    left_one = left_half(1)
    for group in range(groups):
        rhs = summed_parts(ssum_ref, 32 * group, 8, 2, 8)
        diag = summed_parts(ssum_ref, 32 * group + 16, 8, 2, 8)
        last = 32 * groups + 32 * (group // 8) + group % 8
        rhs_last = summed_parts(ssum_ref, last, 1, 2, 8)
        diag_last = summed_parts(ssum_ref, last + 16, 1, 2, 8)
        for half in range(2):
            lanes = slice(half * LANES, (half + 1) * LANES)
            row = 20 * (2 * group + half)
            out_ref[row:row + 8] = jnp.where(left, rhs[:, lanes], swap_halves(diag[:, lanes]))
            out_ref[row + 10:row + 18] = jnp.where(left, swap_halves(rhs[:, lanes]), diag[:, lanes])
            out_ref[row + 8:row + 9] = jnp.where(left_one, rhs_last[:, lanes], swap_halves(diag_last[:, lanes]))
            out_ref[row + 18:row + 19] = jnp.where(left_one, swap_halves(rhs_last[:, lanes]), diag_last[:, lanes])
            owner = 4 * group + 2 * half
            out_ref[row + 9:row + 10] = wanted[owner:owner + 1]
            out_ref[row + 19:row + 20] = wanted[owner + 1:owner + 2]


def apply_kernel(chunk, first, *refs):
    if first:
        (in_ref, camp_ref, jac_ref, index_ref, pointhot_ref, slothot_ref, inverse_ref, damp_ref, precond_ref,
         out_ref, table_ref, last_ref, rz_ref, *work) = refs
    else:
        (in_ref, camp_ref, jac_ref, index_ref, pointhot_ref, slothot_ref, inverse_ref, damp_ref, precond_ref,
         oldtable_ref, oldlast_ref, oldrz_ref, oldown_ref,
         out_ref, own_ref, rz_ref, *work, table_ref, last_ref) = refs
    psum_ref, ssum_ref, solved_ref, along_ref, pointrows_ref, slotrows_ref = work
    nobs = camp_ref.shape[1]
    steps = nobs // chunk
    pairs = table_ref.shape[0]
    groups = pairs // 2
    rz = carried_scalar(in_ref)
    rz_ref[...] = jnp.broadcast_to(rz, rz_ref.shape)
    own = precond_ref[...]
    if not first:
        beta = rz / oldrz_ref[0:1, 0:1]
        own = own + beta * oldown_ref[...]
        own_ref[...] = own
    for pair in range(pairs):
        head, tail = load_five(in_ref, pair)
        if not first:
            head = head + beta * oldtable_ref[pair]
            tail = tail + beta * oldlast_ref[pair:pair + 1]
        table_ref[pair] = head
        last_ref[pair:pair + 1] = tail

    def build_points(step):
        lanes = chunk_lanes(step, chunk)
        for tile in range(chunk // LANES):
            spot = slice(step * chunk + tile * LANES, step * chunk + (tile + 1) * LANES)
            slot = index_ref[2:3, spot]
            low = jnp.broadcast_to(slot & (LANES - 1), (8, LANES))
            high = jnp.broadcast_to(slot >> 7, (8, LANES))
            taken = take_tables([functools.partial(table_ref.__getitem__, pair) for pair in range(pairs)], low, high)
            tail = jnp.zeros((8, LANES), F32)
            for base in range(0, pairs, 8):
                hit = high == iota((8, LANES), 0) + base
                tail = jnp.where(hit, take_lanes(last_ref[base:base + 8], low), tail)
            tail = jnp.sum(tail, axis=0, keepdims=True)
            along_ref[0:1, spot] = jnp.sum(camp_ref[0:8, spot] * taken, axis=0, keepdims=True) + camp_ref[16:17, spot] * tail
            along_ref[1:2, spot] = jnp.sum(camp_ref[8:16, spot] * taken, axis=0, keepdims=True) + camp_ref[17:18, spot] * tail
        sides = wide_parts(two_level(jac_ref[:, lanes], along_ref[0:1, lanes], along_ref[1:2, lanes]), 3)
        rows = [side[place:place + 1] for side in sides for place in (0, 1, 2)]
        pointrows_ref[:, lanes] = stack_tiles(masked_rows(rows, group_hits(index_ref[1:2, lanes])))

    pipelined(steps, build_points, lambda step: add_product(
        psum_ref, pointrows_ref, pointhot_ref, chunk_lanes(step, chunk), step == 0))
    solve_points(inverse_ref, [summed_parts(psum_ref, 8 * place, 8, 3, 24) for place in range(3)], solved_ref)
    energies = []

    def build_slots(step):
        lanes = chunk_lanes(step, chunk)
        kept_a, kept_b = kept_rows(solved_ref, index_ref, jac_ref, along_ref, step * chunk, chunk)
        heads = wide_parts(camp_ref[0:8, lanes] * kept_a + camp_ref[8:16, lanes] * kept_b, 2)
        tails = wide_parts(camp_ref[16:17, lanes] * kept_a + camp_ref[17:18, lanes] * kept_b, 2)
        group = index_ref[3:4, lanes]
        slotrows_ref[:, lanes] = spread_slots([heads], tails, group, groups)
        energy = along_ref[0:1, lanes] * kept_a + along_ref[1:2, lanes] * kept_b
        energies.append(jnp.where(group >= 0, energy, 0.0))

    pipelined(steps, build_slots, lambda step: add_product(
        ssum_ref, slotrows_ref, slothot_ref, chunk_lanes(step, chunk), step == 0))
    energy = energies[0]
    for more in energies[1:]:
        energy = energy + more
    partial = sum_all(energy) + sum_all(damp_ref[...] * own * own)
    for group in range(groups):
        head = summed_parts(ssum_ref, 16 * group, 8, 2, 8)
        tail = summed_parts(ssum_ref, 16 * groups + 16 * (group // 8) + group % 8, 1, 2, 8)
        for half in range(2):
            lanes = slice(half * LANES, (half + 1) * LANES)
            store_five(out_ref, 2 * group + half, head[:, lanes], tail[:, lanes], partial)


def owner_sums(values, ids, cameras):
    groups = cameras // 256
    tiles = []
    for value in values:
        parts = wide_parts(value, 2)
        tiles.append(jnp.concatenate(parts, axis=0).astype(BF16))
    rows = []
    for number in range(groups):
        hit = jnp.where(jnp.broadcast_to(ids >> 8, tiles[0].shape) == number, 1.0, 0.0).astype(BF16)
        rows += [tile * hit for tile in tiles]
    sums = contract(jnp.concatenate(rows, axis=0), one_hot_rows(ids & 255, 256))
    results = []
    height = values[0].shape[0]
    each = 2 * height * len(tiles)
    for place in range(len(values)):
        blocks = []
        for group in range(groups):
            start = group * each + place * 2 * height
            blocks.append(sums[start:start + height] + sums[start + height:start + 2 * height])
        results.append(jnp.concatenate(blocks, axis=1)[0:9])
    return results


def send_wanted(out_ref, precond, ids, scalar):
    cameras = precond.shape[1]
    blocks = cameras // LANES
    spare = [jnp.zeros((1, LANES), F32)] * (8 - blocks)
    last = jnp.concatenate([precond[8:9, block * LANES:(block + 1) * LANES] for block in range(blocks)] + spare, axis=0)
    for pair in range(out_ref.shape[0] // 10):
        own = ids[:, pair * LANES:(pair + 1) * LANES]
        low = jnp.broadcast_to(own & (LANES - 1), (8, LANES))
        high = jnp.broadcast_to(own >> 7, (8, LANES))
        head = take_tables(
            [functools.partial(lambda start: precond[0:8, start:start + LANES], block * LANES) for block in range(blocks)],
            low, high)
        tail = jnp.where(high == iota((8, LANES), 0), take_lanes(last, low), 0.0)
        store_five(out_ref, pair, head, jnp.sum(tail, axis=0, keepdims=True), scalar)


def owner_start_kernel(in_ref, damp_ref, out_ref, residual_ref, scaling_ref, precond_ref, ids_ref):
    rhs, diag, ids = [], [], []
    left = left_half(9)
    for pair in range(in_ref.shape[0] // 20):
        even = in_ref[20 * pair:20 * pair + 9]
        odd = in_ref[20 * pair + 10:20 * pair + 19]
        low = jnp.where(left, even, swap_halves(odd))
        high = jnp.where(left, swap_halves(even), odd)
        pad = jnp.zeros((7, LANES), F32)
        rhs.append(jnp.concatenate([low, pad], axis=0))
        diag.append(jnp.concatenate([high, pad], axis=0))
        even = in_ref[20 * pair + 9:20 * pair + 10]
        odd = in_ref[20 * pair + 19:20 * pair + 20]
        ids.append(jnp.where(left_half(1), even, swap_halves(odd)).astype(jnp.int32))
    ids = jnp.concatenate(ids, axis=1)
    ids_ref[...] = ids
    rhs = jnp.concatenate(rhs, axis=1)
    diag = jnp.concatenate(diag, axis=1)
    residual, diag = owner_sums([rhs, diag], ids, damp_ref.shape[1])
    scaling = diag + damp_ref[...]
    precond = residual / scaling
    residual_ref[...] = residual
    scaling_ref[...] = scaling
    precond_ref[...] = precond
    send_wanted(out_ref, precond, ids, sum_all(residual * precond))


def owner_image(in_ref, ids, cameras):
    image = []
    pad = jnp.zeros((7, LANES), F32)
    for pair in range(in_ref.shape[0] // 10):
        head, tail = load_five(in_ref, pair)
        image.append(jnp.concatenate([head, tail, pad], axis=0))
    return owner_sums([jnp.concatenate(image, axis=1)], ids, cameras)[0]


def owner_middle_kernel(in_ref, ids_ref, rz_ref, damp_ref, direction_ref, residual_ref, scaling_ref,
                        out_ref, update_ref, newres_ref, precond_ref):
    ids = ids_ref[...]
    direction = direction_ref[...]
    image = owner_image(in_ref, ids, damp_ref.shape[1]) + damp_ref[...] * direction
    step = rz_ref[0:1, 0:1] / carried_scalar(in_ref)
    update_ref[...] = step * direction
    residual = residual_ref[...] - step * image
    precond = residual / scaling_ref[...]
    newres_ref[...] = residual
    precond_ref[...] = precond
    send_wanted(out_ref, precond, ids, sum_all(residual * precond))


def owner_end_kernel(in_ref, ids_ref, rz_ref, damp_ref, direction_ref, residual_ref, update_ref,
                     newupdate_ref, newres_ref):
    direction = direction_ref[...]
    image = owner_image(in_ref, ids_ref[...], damp_ref.shape[1]) + damp_ref[...] * direction
    step = rz_ref[0:1, 0:1] / carried_scalar(in_ref)
    newupdate_ref[...] = update_ref[...] + step * direction
    newres_ref[...] = residual_ref[...] - step * image


def call(kernel, outs, scratch, *args, smem=0, hbm=0):
    whole = pl.BlockSpec(memory_space=pltpu.VMEM)
    specs = [pl.BlockSpec(memory_space=pltpu.SMEM)] * smem + [pl.BlockSpec(memory_space=pltpu.HBM)] * hbm
    specs += [whole] * (len(args) - smem - hbm)
    return pl.pallas_call(
        kernel,
        out_shape=[jax.ShapeDtypeStruct(shape, dtype) for shape, dtype in outs],
        in_specs=specs,
        out_specs=[whole] * len(outs),
        scratch_shapes=scratch,
        compiler_params=pltpu.CompilerParams(vmem_limit_bytes=VMEM_BYTES),
    )(*args)


def exchange(blocks, shards):
    moved = lax.all_to_all(blocks.reshape(shards, 1, -1), AXES, split_axis=0, concat_axis=0, tiled=True)
    return moved.reshape(blocks.shape)


def product_scratch(point_rows, slot_rows, nobs):
    return [pltpu.VMEM((rows, nobs), BF16) for rows in (point_rows, slot_rows)]


def start_call(chunk, *args):
    jac_cam, request, cam_damp = args[1], args[6], args[8]
    nobs = jac_cam.shape[1]
    shards = request.shape[0]
    groups = shards * CAP // 256
    copied = args[1:]
    rows = groups * 32 + (groups + 7) // 8 * 32
    scratch = [pltpu.VMEM((224, LANES), F32), pltpu.VMEM((rows, 256), F32), pltpu.VMEM((3, 8, LANES), F32)]
    scratch += product_scratch(224, rows, nobs)
    scratch += [pltpu.VMEM(arg.shape, arg.dtype) for arg in copied[:-1]]
    scratch += [pltpu.SemaphoreType.DMA] * len(copied)
    outs = [((shards * 10, LANES), F32), ((24, nobs), F32), ((8, nobs), F32), ((8, nobs), jnp.int32),
            ((nobs, LANES), BF16), ((nobs, 256), BF16), ((6, 8, LANES), F32), (cam_damp.shape, F32)]
    copied = [pltpu.with_memory_space_constraint(arg, pltpu.HBM) for arg in copied]
    return call(functools.partial(start_kernel, chunk), outs, scratch, args[0], *copied, smem=1, hbm=len(copied))


def apply_call(chunk, first, *args):
    arrived, camp = args[:2]
    nobs = camp.shape[1]
    shards = arrived.shape[0] // 5
    pairs = shards // 2
    groups = shards // 4
    cameras = args[7].shape[1]
    rows = groups * 16 + (groups + 7) // 8 * 16
    scratch = [pltpu.VMEM((80, LANES), F32), pltpu.VMEM((rows, 256), F32), pltpu.VMEM((3, 8, LANES), F32),
               pltpu.VMEM((8, nobs), F32)]
    scratch += product_scratch(80, rows, nobs)
    table = (pairs, 8, LANES)
    last = ((pairs + 7) // 8 * 8, LANES)
    scalar = ((8, LANES), F32)
    sent = ((shards * 5, LANES), F32)
    if first:
        outs = [sent, (table, F32), (last, F32), scalar]
    else:
        outs = [sent, ((9, cameras), F32), scalar]
        scratch += [pltpu.VMEM(table, F32), pltpu.VMEM(last, F32)]
    return call(functools.partial(apply_kernel, chunk, first), outs, scratch, *args)


def body(jac_cam, jac_pt, obs_residual, obs_point, obs_slot, request, obs_count, cam_damp, pt_damp):
    nobs = jac_cam.shape[1]
    shards = request.shape[0]
    cameras = cam_damp.shape[1]
    slots = shards * CAP
    start_chunk, chunk = 512, 256
    own = ((9, cameras), F32)
    sent = ((shards * 5, LANES), F32)
    sums, camp, jac, index, pointhot, slothot, inverse, damp = start_call(
        start_chunk, obs_count, jac_cam, jac_pt, obs_residual, obs_point.reshape(1, nobs), obs_slot.reshape(1, nobs),
        request, pt_damp.reshape(8, LANES), cam_damp)
    arrived = exchange(sums, shards)
    send, residual, scaling, precond, ids = call(
        owner_start_kernel, [sent, own, own, own, ((1, slots), jnp.int32)], [], arrived, damp)
    arrived = exchange(send, shards)
    send, table, last, rz = apply_call(
        chunk, True, arrived, camp, jac, index, pointhot, slothot, inverse, damp, precond)
    arrived = exchange(send, shards)
    direction = precond
    send, update, residual, precond = call(
        owner_middle_kernel, [sent, own, own, own], [],
        arrived, ids, rz, damp, direction, residual, scaling)
    arrived = exchange(send, shards)
    send, direction, rz = apply_call(
        chunk, False, arrived, camp, jac, index, pointhot, slothot, inverse, damp, precond, table, last, rz, direction)
    arrived = exchange(send, shards)
    update, residual = call(
        owner_end_kernel, [own, own], [], arrived, ids, rz, damp, direction, residual, update)
    return update, residual


def solution(mesh):
    wide = P(None, AXES)
    flat = P(AXES)
    return jax.shard_map(
        body,
        mesh=mesh,
        in_specs=(wide, wide, wide, flat, flat, P(AXES, None), flat, wide, flat),
        out_specs=(wide, wide),
        check_vma=False,
    )
```

```python
import functools

import jax
import jax.numpy as jnp
from jax import lax
from jax.experimental import pallas as pl
from jax.experimental.pallas import tpu as pltpu
from jax.sharding import PartitionSpec as P

AXES = ("cell", "img")
F32 = jnp.float32
BF16 = jnp.bfloat16
LANES = 128
CAP = 64
VMEM_BYTES = 32 * 1024 * 1024


def iota(shape, dim):
    return lax.broadcasted_iota(jnp.int32, shape, dim)


def take_lanes(table, lanes):
    return jnp.take_along_axis(table, lanes, axis=1, mode="promise_in_bounds")


def take_tables(tables, low, high):
    bits = (len(tables) - 1).bit_length()
    hits = [(high & (1 << bit)) != 0 for bit in range(bits)]

    def pick(base, bit):
        if bit < 0:
            return take_lanes(tables[base](), low)
        other = base + (1 << bit)
        if other >= len(tables):
            return pick(base, bit - 1)
        return jnp.where(hits[bit], pick(other, bit - 1), pick(base, bit - 1))

    return pick(0, bits - 1)


def contract(left, right):
    return lax.dot_general(left, right, (((1,), (1,)), ((), ())), preferred_element_type=F32)


def one_hot_rows(index, rows):
    hit = iota((rows, index.shape[1]), 0) == index
    return jnp.where(hit, 1.0, 0.0).astype(BF16)


def one_hot_columns(index, columns):
    spread = jnp.broadcast_to(index.astype(F32), (LANES, LANES)).astype(BF16).T
    spread = jnp.concatenate([spread] * (columns // LANES), axis=1)
    lane = iota((LANES, columns), 1).astype(F32).astype(BF16)
    return jnp.where(spread == lane, jnp.ones((), BF16), jnp.zeros((), BF16))


def rounded_parts(value, count):
    parts = []
    for _ in range(count):
        part = value.astype(BF16)
        parts.append(part)
        value = value - part.astype(F32)
    return parts


def masked_rows(rows, hit):
    return [jnp.where(hit, jnp.broadcast_to(row, hit.shape), 0.0) for row in rows]


def stack_tiles(blocks):
    if len(blocks) % 2:
        blocks = blocks + [jnp.zeros_like(blocks[0])]
    return jnp.concatenate(blocks, axis=0).astype(BF16)


def group_hits(group):
    return jnp.broadcast_to(group, (8, group.shape[1])) == iota((8, group.shape[1]), 0)


def spread_slots(heads, tails, group, groups):
    width = group.shape[1]
    tiles = [jnp.concatenate(parts, axis=0).astype(BF16) for parts in heads]
    rows = []
    wide = jnp.broadcast_to(group, (8, width))
    for number in range(groups):
        hit = jnp.where(wide == number, 1.0, 0.0)
        hit = jnp.concatenate([hit, hit], axis=0).astype(BF16)
        rows += [tile * hit for tile in tiles]
    last = []
    for base in range(0, groups, 8):
        hit = wide == iota((8, width), 0) + base
        last += masked_rows(tails, hit)
    return jnp.concatenate(rows + [stack_tiles(last)], axis=0)


def wide_parts(value, count):
    return [part.astype(F32) for part in rounded_parts(value, count)]


def swap_halves(value):
    return pltpu.roll(value, CAP, 1)


def left_half(rows=8):
    return iota((rows, LANES), 1) < CAP


def sum_all(value):
    return jnp.sum(jnp.sum(value, axis=1, keepdims=True), axis=0, keepdims=True)


def carried_scalar(ref):
    total = ref[4:5, :]
    for sender in range(1, ref.shape[0] // 5):
        total = total + ref[5 * sender + 4:5 * sender + 5, :]
    return total[:, CAP:CAP + 1]


def store_five(out_ref, pair, head, tail, scalar):
    left = left_half()
    turned = swap_halves(head)
    even = jnp.where(left, head, pltpu.roll(turned, 4, 0))
    odd = jnp.where(left, turned, pltpu.roll(head, 4, 0))
    last = jnp.broadcast_to(tail, (8, LANES))
    last_even = jnp.where(left, last, scalar)
    last_odd = jnp.where(left, swap_halves(last), scalar)
    out_ref[10 * pair:10 * pair + 4] = even[0:4]
    out_ref[10 * pair + 4:10 * pair + 5] = last_even[0:1]
    out_ref[10 * pair + 5:10 * pair + 9] = odd[0:4]
    out_ref[10 * pair + 9:10 * pair + 10] = last_odd[0:1]


def load_five(in_ref, pair):
    left = left_half(4)
    even = in_ref[10 * pair:10 * pair + 4]
    odd = in_ref[10 * pair + 5:10 * pair + 9]
    low = jnp.where(left, even, swap_halves(odd))
    high = jnp.where(left, swap_halves(even), odd)
    last_even = in_ref[10 * pair + 4:10 * pair + 5]
    last_odd = in_ref[10 * pair + 9:10 * pair + 10]
    tail = jnp.where(left_half(1), last_even, swap_halves(last_odd))
    return jnp.concatenate([low, high], axis=0), tail


def pipelined(steps, build, product):
    for step in range(steps):
        build(step)
        product(step)


def chunk_lanes(step, chunk):
    return slice(step * chunk, (step + 1) * chunk)


def add_product(sums_ref, left_ref, right_ref, lanes, first):
    product = jnp.dot(left_ref[:, lanes], right_ref[lanes, :], preferred_element_type=F32)
    if first:
        sums_ref[...] = product
    else:
        sums_ref[...] += product


def point_spread(solved_ref, low, group, jac):
    low = jnp.broadcast_to(low, (8, LANES))
    hit = group_hits(group)
    first = jnp.zeros((8, LANES), F32)
    second = jnp.zeros((8, LANES), F32)
    for axis in range(3):
        taken = jnp.where(hit, take_lanes(solved_ref[axis], low), 0.0)
        first = first + jac[axis:axis + 1] * taken
        second = second + jac[axis + 4:axis + 5] * taken
    return jnp.sum(first, axis=0, keepdims=True), jnp.sum(second, axis=0, keepdims=True)


def two_level(jac, first, second):
    both = jac * jnp.where(iota(jac.shape, 0) < 4, first, second)
    return both + pltpu.roll(both, 4, 0)


def kept_rows(solved_ref, index_ref, jac_ref, along_ref, start, chunk):
    kept_a, kept_b = [], []
    for tile in range(chunk // LANES):
        spot = slice(start + tile * LANES, start + (tile + 1) * LANES)
        first, second = point_spread(solved_ref, index_ref[0:1, spot], index_ref[1:2, spot], jac_ref[:, spot])
        kept_a.append(along_ref[0:1, spot] - first)
        kept_b.append(along_ref[1:2, spot] - second)
    return jnp.concatenate(kept_a, axis=1), jnp.concatenate(kept_b, axis=1)


def solve_points(inverse_ref, totals, solved_ref):
    rows = ((0, 3, 5), (3, 1, 4), (5, 4, 2))
    for axis in range(3):
        solved_ref[axis] = (
            inverse_ref[rows[axis][0]] * totals[0]
            + inverse_ref[rows[axis][1]] * totals[1]
            + inverse_ref[rows[axis][2]] * totals[2]
        )


def summed_parts(sums_ref, start, rows, count, step):
    total = sums_ref[start:start + rows, :]
    for part in range(1, count):
        begin = start + part * step
        total = total + sums_ref[begin:begin + rows, :]
    return total


def start_kernel(chunk, count_ref, cam_hbm, pt_hbm, err_hbm, point_hbm, slot_hbm, req_hbm, damp_hbm, camdamp_hbm,
                 out_ref, camp_ref, jac_ref, index_ref, pointhot_ref, slothot_ref, inverse_ref, camdamp_ref,
                 psum_ref, ssum_ref, solved_ref, pointrows_ref, slotrows_ref,
                 cam_ref, pt_ref, err_ref, point_ref, slot_ref, req_ref, damp_ref,
                 cam_sem, pt_sem, err_sem, point_sem, slot_sem, req_sem, damp_sem, camdamp_sem):
    nobs = cam_ref.shape[1]
    steps = nobs // chunk
    copies = [
        pltpu.make_async_copy(point_hbm, point_ref, point_sem),
        pltpu.make_async_copy(slot_hbm, slot_ref, slot_sem),
        pltpu.make_async_copy(pt_hbm, pt_ref, pt_sem),
        pltpu.make_async_copy(err_hbm, err_ref, err_sem),
        pltpu.make_async_copy(damp_hbm, damp_ref, damp_sem),
        pltpu.make_async_copy(cam_hbm, cam_ref, cam_sem),
        pltpu.make_async_copy(req_hbm, req_ref, req_sem),
        pltpu.make_async_copy(camdamp_hbm, camdamp_ref, camdamp_sem),
    ]
    for copy in copies:
        copy.start()
    count = count_ref[0]
    groups = req_ref.shape[0] * CAP // 256
    for copy in copies[:2]:
        copy.wait()

    for step in range(steps):
        lanes = chunk_lanes(step, chunk)
        live = iota((1, chunk), 1) + step * chunk < count
        point = point_ref[:, lanes]
        low = point & (LANES - 1)
        group = jnp.where(live, point >> 7, -1)
        slot = slot_ref[:, lanes]
        index_ref[0:1, lanes] = low
        index_ref[1:2, lanes] = group
        index_ref[2:3, lanes] = slot
        index_ref[3:4, lanes] = jnp.where(live, slot >> 8, -1)
        for tile in range(chunk // LANES):
            spot = slice(step * chunk + tile * LANES, step * chunk + (tile + 1) * LANES)
            part = chunk_lanes(tile, LANES)
            pointhot_ref[spot, :] = one_hot_columns(low[:, part], LANES)
            slothot_ref[spot, :] = one_hot_columns(slot[:, part] & 255, 256)
    for copy in copies[2:5]:
        copy.wait()

    def build_points(step):
        lanes = chunk_lanes(step, chunk)
        group = index_ref[1:2, lanes]
        jac = pt_ref[:, lanes]
        zero = jnp.zeros((1, chunk), F32)
        jac_ref[:, lanes] = jnp.concatenate([jac[0:3], zero, jac[3:6], zero], axis=0)
        jac_a = jnp.concatenate([jac[0:3], zero, jac[0:3], zero], axis=0)
        jac_b = jnp.concatenate([jac[3:6], zero, jac[3:6], zero], axis=0)
        turn_a = jnp.concatenate([jac[0:3], zero, jac[1:3], jac[0:1], zero], axis=0)
        turn_b = jnp.concatenate([jac[3:6], zero, jac[4:6], jac[3:4], zero], axis=0)
        err = err_ref[:, lanes]
        blocks = wide_parts(jac_a * turn_a + jac_b * turn_b, 3)
        sides = wide_parts(jac_a * err[0:1] + jac_b * err[1:2], 3)
        rows = [block[place:place + 1] for block in blocks for place in (0, 1, 2, 4, 5, 6)]
        rows += [side[place:place + 1] for side in sides for place in (0, 1, 2)]
        pointrows_ref[:, lanes] = stack_tiles(masked_rows(rows, group_hits(group)))

    pipelined(steps, build_points, lambda step: add_product(
        psum_ref, pointrows_ref, pointhot_ref, chunk_lanes(step, chunk), step == 0))

    damp = damp_ref[...]
    m00, m11, m22, m01, m12, m20 = [summed_parts(psum_ref, 8 * place, 8, 3, 48) for place in range(6)]
    m00, m11, m22 = m00 + damp, m11 + damp, m22 + damp
    c00 = m11 * m22 - m12 * m12
    c01 = m12 * m20 - m01 * m22
    c02 = m01 * m12 - m11 * m20
    c11 = m22 * m00 - m20 * m20
    c12 = m20 * m01 - m12 * m00
    c22 = m00 * m11 - m01 * m01
    det = m00 * c00 + m01 * c01 + m20 * c02
    for place, cofactor in enumerate((c00, c11, c22, c01, c12, c02)):
        inverse_ref[place] = cofactor / det
    solve_points(inverse_ref, [summed_parts(psum_ref, 144 + 8 * place, 8, 3, 24) for place in range(3)], solved_ref)
    for copy in copies[5:]:
        copy.wait()

    def build_slots(step):
        lanes = chunk_lanes(step, chunk)
        cam_a = cam_ref[0:8, lanes]
        cam_b = cam_ref[9:17, lanes]
        last = jnp.concatenate([cam_ref[8:9, lanes], cam_ref[17:18, lanes], jnp.zeros((6, chunk), F32)], axis=0)
        camp_ref[0:8, lanes] = cam_a
        camp_ref[8:16, lanes] = cam_b
        camp_ref[16:24, lanes] = last
        kept_a, kept_b = kept_rows(solved_ref, index_ref, jac_ref, err_ref, step * chunk, chunk)
        rhs = wide_parts(-(cam_a * kept_a + cam_b * kept_b), 2)
        diag = wide_parts(cam_a * cam_a + cam_b * cam_b, 2)
        last_a, last_b = last[0:1], last[1:2]
        tails = wide_parts(-(last_a * kept_a + last_b * kept_b), 2) + wide_parts(last_a * last_a + last_b * last_b, 2)
        slotrows_ref[:, lanes] = spread_slots([rhs, diag], tails, index_ref[3:4, lanes], groups)

    pipelined(steps, build_slots, lambda step: add_product(
        ssum_ref, slotrows_ref, slothot_ref, chunk_lanes(step, chunk), step == 0))
    wanted = req_ref[...].astype(F32)
    wanted = jnp.concatenate([wanted, jnp.zeros_like(wanted)], axis=1)
    left = left_half()
    left_one = left_half(1)
    for group in range(groups):
        rhs = summed_parts(ssum_ref, 32 * group, 8, 2, 8)
        diag = summed_parts(ssum_ref, 32 * group + 16, 8, 2, 8)
        last = 32 * groups + 32 * (group // 8) + group % 8
        rhs_last = summed_parts(ssum_ref, last, 1, 2, 8)
        diag_last = summed_parts(ssum_ref, last + 16, 1, 2, 8)
        for half in range(2):
            lanes = slice(half * LANES, (half + 1) * LANES)
            row = 20 * (2 * group + half)
            out_ref[row:row + 8] = jnp.where(left, rhs[:, lanes], swap_halves(diag[:, lanes]))
            out_ref[row + 10:row + 18] = jnp.where(left, swap_halves(rhs[:, lanes]), diag[:, lanes])
            out_ref[row + 8:row + 9] = jnp.where(left_one, rhs_last[:, lanes], swap_halves(diag_last[:, lanes]))
            out_ref[row + 18:row + 19] = jnp.where(left_one, swap_halves(rhs_last[:, lanes]), diag_last[:, lanes])
            owner = 4 * group + 2 * half
            out_ref[row + 9:row + 10] = wanted[owner:owner + 1]
            out_ref[row + 19:row + 20] = wanted[owner + 1:owner + 2]


def apply_kernel(chunk, first, *refs):
    if first:
        (in_ref, camp_ref, jac_ref, index_ref, pointhot_ref, slothot_ref, inverse_ref, damp_ref, precond_ref,
         out_ref, table_ref, last_ref, rz_ref, *work) = refs
    else:
        (in_ref, camp_ref, jac_ref, index_ref, pointhot_ref, slothot_ref, inverse_ref, damp_ref, precond_ref,
         oldtable_ref, oldlast_ref, oldrz_ref, oldown_ref,
         out_ref, own_ref, rz_ref, *work, table_ref, last_ref) = refs
    psum_ref, ssum_ref, solved_ref, along_ref, pointrows_ref, slotrows_ref = work
    nobs = camp_ref.shape[1]
    steps = nobs // chunk
    pairs = table_ref.shape[0]
    groups = pairs // 2
    rz = carried_scalar(in_ref)
    rz_ref[...] = jnp.broadcast_to(rz, rz_ref.shape)
    own = precond_ref[...]
    if not first:
        beta = rz / oldrz_ref[0:1, 0:1]
        own = own + beta * oldown_ref[...]
        own_ref[...] = own
    for pair in range(pairs):
        head, tail = load_five(in_ref, pair)
        if not first:
            head = head + beta * oldtable_ref[pair]
            tail = tail + beta * oldlast_ref[pair:pair + 1]
        table_ref[pair] = head
        last_ref[pair:pair + 1] = tail

    def build_points(step):
        lanes = chunk_lanes(step, chunk)
        for tile in range(chunk // LANES):
            spot = slice(step * chunk + tile * LANES, step * chunk + (tile + 1) * LANES)
            slot = index_ref[2:3, spot]
            low = jnp.broadcast_to(slot & (LANES - 1), (8, LANES))
            high = jnp.broadcast_to(slot >> 7, (8, LANES))
            taken = take_tables([functools.partial(table_ref.__getitem__, pair) for pair in range(pairs)], low, high)
            tail = jnp.zeros((8, LANES), F32)
            for base in range(0, pairs, 8):
                hit = high == iota((8, LANES), 0) + base
                tail = jnp.where(hit, take_lanes(last_ref[base:base + 8], low), tail)
            tail = jnp.sum(tail, axis=0, keepdims=True)
            along_ref[0:1, spot] = jnp.sum(camp_ref[0:8, spot] * taken, axis=0, keepdims=True) + camp_ref[16:17, spot] * tail
            along_ref[1:2, spot] = jnp.sum(camp_ref[8:16, spot] * taken, axis=0, keepdims=True) + camp_ref[17:18, spot] * tail
        sides = wide_parts(two_level(jac_ref[:, lanes], along_ref[0:1, lanes], along_ref[1:2, lanes]), 3)
        rows = [side[place:place + 1] for side in sides for place in (0, 1, 2)]
        pointrows_ref[:, lanes] = stack_tiles(masked_rows(rows, group_hits(index_ref[1:2, lanes])))

    pipelined(steps, build_points, lambda step: add_product(
        psum_ref, pointrows_ref, pointhot_ref, chunk_lanes(step, chunk), step == 0))
    solve_points(inverse_ref, [summed_parts(psum_ref, 8 * place, 8, 3, 24) for place in range(3)], solved_ref)
    energies = []

    def build_slots(step):
        lanes = chunk_lanes(step, chunk)
        kept_a, kept_b = kept_rows(solved_ref, index_ref, jac_ref, along_ref, step * chunk, chunk)
        heads = wide_parts(camp_ref[0:8, lanes] * kept_a + camp_ref[8:16, lanes] * kept_b, 2)
        tails = wide_parts(camp_ref[16:17, lanes] * kept_a + camp_ref[17:18, lanes] * kept_b, 2)
        group = index_ref[3:4, lanes]
        slotrows_ref[:, lanes] = spread_slots([heads], tails, group, groups)
        energy = along_ref[0:1, lanes] * kept_a + along_ref[1:2, lanes] * kept_b
        energies.append(jnp.where(group >= 0, energy, 0.0))

    pipelined(steps, build_slots, lambda step: add_product(
        ssum_ref, slotrows_ref, slothot_ref, chunk_lanes(step, chunk), step == 0))
    energy = energies[0]
    for more in energies[1:]:
        energy = energy + more
    partial = sum_all(energy) + sum_all(damp_ref[...] * own * own)
    for group in range(groups):
        head = summed_parts(ssum_ref, 16 * group, 8, 2, 8)
        tail = summed_parts(ssum_ref, 16 * groups + 16 * (group // 8) + group % 8, 1, 2, 8)
        for half in range(2):
            lanes = slice(half * LANES, (half + 1) * LANES)
            store_five(out_ref, 2 * group + half, head[:, lanes], tail[:, lanes], partial)


def owner_sums(values, ids, cameras):
    groups = cameras // 256
    tiles = []
    for value in values:
        parts = wide_parts(value, 2)
        tiles.append(jnp.concatenate(parts, axis=0).astype(BF16))
    rows = []
    for number in range(groups):
        hit = jnp.where(jnp.broadcast_to(ids >> 8, tiles[0].shape) == number, 1.0, 0.0).astype(BF16)
        rows += [tile * hit for tile in tiles]
    sums = contract(jnp.concatenate(rows, axis=0), one_hot_rows(ids & 255, 256))
    results = []
    height = values[0].shape[0]
    each = 2 * height * len(tiles)
    for place in range(len(values)):
        blocks = []
        for group in range(groups):
            start = group * each + place * 2 * height
            blocks.append(sums[start:start + height] + sums[start + height:start + 2 * height])
        results.append(jnp.concatenate(blocks, axis=1)[0:9])
    return results


def send_wanted(out_ref, precond, ids, scalar):
    cameras = precond.shape[1]
    blocks = cameras // LANES
    spare = [jnp.zeros((1, LANES), F32)] * (8 - blocks)
    last = jnp.concatenate([precond[8:9, block * LANES:(block + 1) * LANES] for block in range(blocks)] + spare, axis=0)
    for pair in range(out_ref.shape[0] // 10):
        own = ids[:, pair * LANES:(pair + 1) * LANES]
        low = jnp.broadcast_to(own & (LANES - 1), (8, LANES))
        high = jnp.broadcast_to(own >> 7, (8, LANES))
        head = take_tables(
            [functools.partial(lambda start: precond[0:8, start:start + LANES], block * LANES) for block in range(blocks)],
            low, high)
        tail = jnp.where(high == iota((8, LANES), 0), take_lanes(last, low), 0.0)
        store_five(out_ref, pair, head, jnp.sum(tail, axis=0, keepdims=True), scalar)


def owner_start_kernel(in_ref, damp_ref, out_ref, residual_ref, scaling_ref, precond_ref, ids_ref):
    rhs, diag, ids = [], [], []
    left = left_half(9)
    for pair in range(in_ref.shape[0] // 20):
        even = in_ref[20 * pair:20 * pair + 9]
        odd = in_ref[20 * pair + 10:20 * pair + 19]
        low = jnp.where(left, even, swap_halves(odd))
        high = jnp.where(left, swap_halves(even), odd)
        pad = jnp.zeros((7, LANES), F32)
        rhs.append(jnp.concatenate([low, pad], axis=0))
        diag.append(jnp.concatenate([high, pad], axis=0))
        even = in_ref[20 * pair + 9:20 * pair + 10]
        odd = in_ref[20 * pair + 19:20 * pair + 20]
        ids.append(jnp.where(left_half(1), even, swap_halves(odd)).astype(jnp.int32))
    ids = jnp.concatenate(ids, axis=1)
    ids_ref[...] = ids
    rhs = jnp.concatenate(rhs, axis=1)
    diag = jnp.concatenate(diag, axis=1)
    residual, diag = owner_sums([rhs, diag], ids, damp_ref.shape[1])
    scaling = diag + damp_ref[...]
    precond = residual / scaling
    residual_ref[...] = residual
    scaling_ref[...] = scaling
    precond_ref[...] = precond
    send_wanted(out_ref, precond, ids, sum_all(residual * precond))


def owner_image(in_ref, ids, cameras):
    image = []
    pad = jnp.zeros((7, LANES), F32)
    for pair in range(in_ref.shape[0] // 10):
        head, tail = load_five(in_ref, pair)
        image.append(jnp.concatenate([head, tail, pad], axis=0))
    return owner_sums([jnp.concatenate(image, axis=1)], ids, cameras)[0]


def owner_middle_kernel(in_ref, ids_ref, rz_ref, damp_ref, direction_ref, residual_ref, scaling_ref,
                        out_ref, update_ref, newres_ref, precond_ref):
    ids = ids_ref[...]
    direction = direction_ref[...]
    image = owner_image(in_ref, ids, damp_ref.shape[1]) + damp_ref[...] * direction
    step = rz_ref[0:1, 0:1] / carried_scalar(in_ref)
    update_ref[...] = step * direction
    residual = residual_ref[...] - step * image
    precond = residual / scaling_ref[...]
    newres_ref[...] = residual
    precond_ref[...] = precond
    send_wanted(out_ref, precond, ids, sum_all(residual * precond))


def owner_end_kernel(in_ref, ids_ref, rz_ref, damp_ref, direction_ref, residual_ref, update_ref,
                     newupdate_ref, newres_ref):
    direction = direction_ref[...]
    image = owner_image(in_ref, ids_ref[...], damp_ref.shape[1]) + damp_ref[...] * direction
    step = rz_ref[0:1, 0:1] / carried_scalar(in_ref)
    newupdate_ref[...] = update_ref[...] + step * direction
    newres_ref[...] = residual_ref[...] - step * image


def call(kernel, outs, scratch, *args, smem=0, hbm=0):
    whole = pl.BlockSpec(memory_space=pltpu.VMEM)
    specs = [pl.BlockSpec(memory_space=pltpu.SMEM)] * smem + [pl.BlockSpec(memory_space=pltpu.HBM)] * hbm
    specs += [whole] * (len(args) - smem - hbm)
    return pl.pallas_call(
        kernel,
        out_shape=[jax.ShapeDtypeStruct(shape, dtype) for shape, dtype in outs],
        in_specs=specs,
        out_specs=[whole] * len(outs),
        scratch_shapes=scratch,
        compiler_params=pltpu.CompilerParams(vmem_limit_bytes=VMEM_BYTES),
    )(*args)


def exchange(blocks, shards):
    moved = lax.all_to_all(blocks.reshape(shards, 1, -1), AXES, split_axis=0, concat_axis=0, tiled=True)
    return moved.reshape(blocks.shape)


def product_scratch(point_rows, slot_rows, nobs):
    return [pltpu.VMEM((rows, nobs), BF16) for rows in (point_rows, slot_rows)]


def start_call(chunk, *args):
    jac_cam, request, cam_damp = args[1], args[6], args[8]
    nobs = jac_cam.shape[1]
    shards = request.shape[0]
    groups = shards * CAP // 256
    copied = args[1:]
    rows = groups * 32 + (groups + 7) // 8 * 32
    scratch = [pltpu.VMEM((224, LANES), F32), pltpu.VMEM((rows, 256), F32), pltpu.VMEM((3, 8, LANES), F32)]
    scratch += product_scratch(224, rows, nobs)
    scratch += [pltpu.VMEM(arg.shape, arg.dtype) for arg in copied[:-1]]
    scratch += [pltpu.SemaphoreType.DMA] * len(copied)
    outs = [((shards * 10, LANES), F32), ((24, nobs), F32), ((8, nobs), F32), ((8, nobs), jnp.int32),
            ((nobs, LANES), BF16), ((nobs, 256), BF16), ((6, 8, LANES), F32), (cam_damp.shape, F32)]
    copied = [pltpu.with_memory_space_constraint(arg, pltpu.HBM) for arg in copied]
    return call(functools.partial(start_kernel, chunk), outs, scratch, args[0], *copied, smem=1, hbm=len(copied))


def apply_call(chunk, first, *args):
    arrived, camp = args[:2]
    nobs = camp.shape[1]
    shards = arrived.shape[0] // 5
    pairs = shards // 2
    groups = shards // 4
    cameras = args[7].shape[1]
    rows = groups * 16 + (groups + 7) // 8 * 16
    scratch = [pltpu.VMEM((80, LANES), F32), pltpu.VMEM((rows, 256), F32), pltpu.VMEM((3, 8, LANES), F32),
               pltpu.VMEM((8, nobs), F32)]
    scratch += product_scratch(80, rows, nobs)
    table = (pairs, 8, LANES)
    last = ((pairs + 7) // 8 * 8, LANES)
    scalar = ((8, LANES), F32)
    sent = ((shards * 5, LANES), F32)
    if first:
        outs = [sent, (table, F32), (last, F32), scalar]
    else:
        outs = [sent, ((9, cameras), F32), scalar]
        scratch += [pltpu.VMEM(table, F32), pltpu.VMEM(last, F32)]
    return call(functools.partial(apply_kernel, chunk, first), outs, scratch, *args)


def body(jac_cam, jac_pt, obs_residual, obs_point, obs_slot, request, obs_count, cam_damp, pt_damp):
    nobs = jac_cam.shape[1]
    shards = request.shape[0]
    cameras = cam_damp.shape[1]
    slots = shards * CAP
    start_chunk, chunk = 512, 256
    own = ((9, cameras), F32)
    sent = ((shards * 5, LANES), F32)
    sums, camp, jac, index, pointhot, slothot, inverse, damp = start_call(
        start_chunk, obs_count, jac_cam, jac_pt, obs_residual, obs_point.reshape(1, nobs), obs_slot.reshape(1, nobs),
        request, pt_damp.reshape(8, LANES), cam_damp)
    arrived = exchange(sums, shards)
    send, residual, scaling, precond, ids = call(
        owner_start_kernel, [sent, own, own, own, ((1, slots), jnp.int32)], [], arrived, damp)
    arrived = exchange(send, shards)
    send, table, last, rz = apply_call(
        chunk, True, arrived, camp, jac, index, pointhot, slothot, inverse, damp, precond)
    arrived = exchange(send, shards)
    direction = precond
    send, update, residual, precond = call(
        owner_middle_kernel, [sent, own, own, own], [],
        arrived, ids, rz, damp, direction, residual, scaling)
    arrived = exchange(send, shards)
    send, direction, rz = apply_call(
        chunk, False, arrived, camp, jac, index, pointhot, slothot, inverse, damp, precond, table, last, rz, direction)
    arrived = exchange(send, shards)
    update, residual = call(
        owner_end_kernel, [own, own], [], arrived, ids, rz, damp, direction, residual, update)
    return update, residual


def solution(mesh):
    wide = P(None, AXES)
    flat = P(AXES)
    return jax.shard_map(
        body,
        mesh=mesh,
        in_specs=(wide, wide, wide, flat, flat, P(AXES, None), flat, wide, flat),
        out_specs=(wide, wide),
        check_vma=False,
    )
```
